32 devices in a mesh: rep: 2 (over y), seq: 4 (over z), tp: 2 (over x), sub: 2 (over core).
Axes of the slice: x: 2, y: 2, z: 4, core: 2. Of those that a mesh axis runs over, the one named last changes fastest.
Arguments:
- latents: bfloat16 [3072, 3072], P(('rep', 'seq')), parts along dimension 0, may hold values from -6 to 6
- w_qkv: bfloat16 [3072, 3, 24, 128], P('seq', None, ('tp', 'sub')), may hold values from -0.109375 to 0.109375
- w_out: bfloat16 [24, 128, 3072], P(('tp', 'sub'), None, 'seq'), may hold values from -0.15625 to 0.15625
- query_gain: float32 [128], replicated, may hold values from 1.5 to 20
- key_gain: float32 [128], replicated, may hold values from 1.5 to 20
- mod_shift: float32 [6144], P('rep'), parts along dimension 0, may hold values from -3 to 3
- mod_scale: float32 [6144], P('rep'), parts along dimension 0, may hold values from -0.5 to 0.5
- mod_gate: float32 [6144], P('rep'), parts along dimension 0, may hold values from 0.5 to 1.5
- block_list: int32 [8, 9], P(('rep', 'seq')), parts along dimension 0, may hold values from 0 to 3, as said below
- block_live: int32 [8, 9], P(('rep', 'seq')), parts along dimension 0, may hold values from 0 to 1, as said below
- key_valid: int32 [3072], P(('rep', 'seq')), parts along dimension 0, may hold values from 0 to 1, as said below
Outputs:
- block_out: bfloat16 [3072, 3072], P(('rep', 'seq'), ('tp', 'sub')), parts along dimension 0
The draws below stay inside these ranges and needn't reach their ends.
There are 2 independent parts, one for each index of `rep`. The reference program is written for one: setup_inputs(seed, part) draws one part's arguments, and reference() takes and returns one part's arrays. A program takes and returns all parts, laid end to end along the dimension named above; an argument that names none is the same for every part. Nothing has to cross between parts.
Inputs may be any that keep to these rules, and one draw needn't show every extreme that they name: `block_list`: tiles are numbered frame by frame, 2 tiles to a frame of tiles. Row a lists, in a drawn order, the tiles within 1 frames of tiles and 1 tile column of tile a; entries outside the video or dropped have block_live 0, and those outside the video repeat a. Live entries are distinct, and a itself is always live. `block_live`: see block_list. `key_valid`: within each tile either all tokens are real or the last 144 are padding.
All inputs are finite; a program needn't handle non-finite values.
Results may differ from the reference program's by a relative error of at most 0.012.
The reference program's roundings to bfloat16 on the way count: a program that leaves them out, or rounds other values in their place, can miss the bound.
Values may be sent and summed in bfloat16 or wider, within the bound.
No kernel may reach another device: no remote copies, remote signals or barrier semaphores. Data moves between devices by JAX's collectives and lax.ppermute only.
A program may use at most 128 MiB of HBM per device.

```python
import math
import jax
import jax.numpy as jnp
from jax import lax

D = 3072
H = 24
HD = 128
TILE = 384
TILES = 4
TOKENS = 1536
GW = 2
GT = 2
RT = 1
WIN = 9
N_TP = 2
N_SUB = 2


def tile_windows(key):
    tile_ids = jnp.arange(TILES, dtype=jnp.int32)
    frame_of = tile_ids // GW
    column_of = tile_ids % GW
    step_frame = jnp.repeat(jnp.arange(-RT, RT + 1, dtype=jnp.int32), 3)
    step_column = jnp.tile(jnp.arange(-1, 2, dtype=jnp.int32), 2 * RT + 1)
    frames = frame_of[:, None] + step_frame[None, :]
    columns = column_of[:, None] + step_column[None, :]
    inside = (frames >= 0) & (frames < GT) & (columns >= 0) & (columns < GW)
    listed = jnp.where(inside, frames * GW + columns, tile_ids[:, None])
    centre = ((step_frame == 0) & (step_column == 0))[None, :]
    keep_draw = jax.random.randint(jax.random.fold_in(key, 11), (TILES, WIN), 0, 4)
    live = inside & ((keep_draw > 0) | centre)
    order_keys = jax.random.randint(jax.random.fold_in(key, 12), (TILES, WIN), 0, 1 << 20) * WIN + jnp.arange(WIN, dtype=jnp.int32)[None, :]
    order = jnp.argsort(order_keys, axis=1)
    listed = jnp.take_along_axis(listed, order, axis=1)
    live = jnp.take_along_axis(live.astype(jnp.int32), order, axis=1)
    return (listed.astype(jnp.int32), live.astype(jnp.int32))


def draw_block_list(key, part):
    return tile_windows(key)[0]


def draw_block_live(key, part):
    return tile_windows(key)[1]


def draw_key_valid(key, part):
    padded = 3 * jax.random.randint(jax.random.fold_in(key, 13), (TILES,), 0, 2)
    position = jnp.arange(TILE, dtype=jnp.int32)
    valid = position[None, :] < (TILE - padded * (TILE // 8))[:, None]
    return valid.astype(jnp.int32).reshape(TOKENS)


def gain_draw(key, salt):
    base = jax.random.uniform(jax.random.fold_in(key, salt), (HD,), jnp.float32, 1.5, 3.0)
    return base


def draw_query_gain(key, part):
    return gain_draw(key, 1)


def draw_key_gain(key, part):
    return gain_draw(key, 2)


def spiked(array, key, source, target, blocks, factor):
    def block_of(axis_at):
        return (jnp.arange(array.shape[axis_at]) // (array.shape[axis_at] // blocks)).reshape((-1,) + (1,) * (array.ndim - 1 - axis_at))

    one_side = jax.random.permutation(key, blocks)[block_of(target)]
    second = (block_of(target) + blocks // 2) % blocks
    return jnp.where((block_of(source) == one_side) | (block_of(source) == second), factor * array, array)


def steps_of(rng, extent, shards, low, top_value):
    def one(dim, shards_of):
        steps = jax.random.uniform(jax.random.fold_in(jax.random.fold_in(rng, 6), dim), (shards_of,), jnp.float32, low / len(shards), top_value / len(shards))
        return jnp.repeat(jnp.exp(steps), extent[dim] // shards_of).reshape((-1,) + (1,) * (len(extent) - dim - 1))

    level = one(*shards[0])
    for cut in shards[1:]:
        level = level * one(*cut)
    return level


def noise(rng, extent, scale, reach, cuts=(), held_as=jnp.bfloat16):
    values = scale * jax.random.normal(rng, extent, jnp.float32)
    if cuts:
        values = values * steps_of(rng, extent, cuts, -0.22, 0.18)
    return jnp.clip(values, -reach, reach).astype(held_as)


def heavy_noise(key, dims, width, reach, cuts, heavy, held_as=jnp.bfloat16):
    array = width * jax.random.normal(key, dims, jnp.float32)
    if cuts:
        array = array * steps_of(key, dims, cuts, -0.22, 0.18)
    return jnp.clip(spiked(array, jax.random.fold_in(key, 3), *heavy), -reach, reach).astype(held_as)


def setup_inputs(seed: int = 0, part: int = 0) -> dict:
    keys = jax.random.split(jax.random.key(seed), 12)
    part_keys = jax.random.split(jax.random.fold_in(keys[11], part), 12)
    latents = noise(part_keys[0], (TOKENS, D), 1.0, 6.0, ((0, 4),))
    w_qkv = noise(keys[1], (D, 3, H, HD), D ** -0.5, 0.109375, ((0, 4), (2, 4)))
    w_out = heavy_noise(keys[2], (H, HD, D), (H * HD) ** -0.5, 0.15625, ((0, 4), (2, 4)), (0, 2, 4, 2.0))
    query_gain = draw_query_gain(jax.random.fold_in(keys[11], 71), part)
    key_gain = draw_key_gain(jax.random.fold_in(keys[11], 71), part)
    mod_shift = noise(part_keys[5], (D,), 0.5, 3.0, (), jnp.float32)
    mod_scale = jnp.clip(jax.random.uniform(part_keys[6], (D,), jnp.float32, -0.5, 0.5), -0.5, 0.5)
    mod_gate = jnp.clip(jax.random.uniform(part_keys[7], (D,), jnp.float32, 0.5, 1.5), 0.5, 1.5)
    block_list = draw_block_list(jax.random.fold_in(jax.random.fold_in(keys[11], part), 71), part)
    block_live = draw_block_live(jax.random.fold_in(jax.random.fold_in(keys[11], part), 71), part)
    key_valid = draw_key_valid(jax.random.fold_in(jax.random.fold_in(keys[11], part), 71), part)
    return {"latents": latents, "w_qkv": w_qkv, "w_out": w_out, "query_gain": query_gain, "key_gain": key_gain, "mod_shift": mod_shift, "mod_scale": mod_scale, "mod_gate": mod_gate, "block_list": block_list, "block_live": block_live, "key_valid": key_valid}


def modulate(latents, mod_shift, mod_scale):
    x_float = latents.astype(jnp.float32)
    centre = x_float - lax.optimization_barrier(jnp.mean(x_float, axis=-1, keepdims=True))
    spread = lax.optimization_barrier(jnp.mean(centre * centre, axis=-1, keepdims=True))
    return (centre * lax.rsqrt(spread + 1e-06) * (1.0 + mod_scale) + mod_shift).astype(jnp.bfloat16)

def head_norm(raw_heads, gain):
    square = lax.optimization_barrier(jnp.mean(raw_heads * raw_heads, axis=-1, keepdims=True))
    return (raw_heads * lax.rsqrt(square + 1e-06) * gain).astype(jnp.bfloat16)

def reference(latents, w_qkv, w_out, query_gain, key_gain, mod_shift, mod_scale, mod_gate, block_list, block_live, key_valid):
    normed = modulate(latents, mod_shift, mod_scale)
    qkv = jnp.dot(normed, w_qkv.reshape(D, 3 * H * HD), preferred_element_type=jnp.float32).reshape(TOKENS, 3, H, HD)
    queries = head_norm(qkv[:, 0], query_gain)
    key_rows = head_norm(qkv[:, 1], key_gain)
    values = qkv[:, 2].astype(jnp.bfloat16)
    tile_ids = jnp.arange(TILES, dtype=jnp.int32)
    tile_pairs = jnp.any((block_list[:, :, None] == tile_ids[None, None, :]) & (block_live[:, :, None] > 0), axis=1)
    key_tile = jnp.arange(TOKENS, dtype=jnp.int32) // TILE
    key_ok = key_valid > 0
    score_scale = 1.0 / math.sqrt(HD)

    def attend_one(index_flat):
        tile_idx = index_flat // H
        head = index_flat % H
        q_tile = lax.dynamic_slice_in_dim(queries, (tile_idx * TILE).astype(jnp.int32), TILE, 0)
        q_head = lax.dynamic_index_in_dim(q_tile, head, 1, keepdims=False)
        k_head = lax.dynamic_index_in_dim(key_rows, head, 1, keepdims=False)
        v_head = lax.dynamic_index_in_dim(values, head, 1, keepdims=False)
        scores = jnp.dot(q_head, k_head.T, preferred_element_type=jnp.float32) * score_scale
        pair_row = lax.dynamic_index_in_dim(tile_pairs, tile_idx, 0, keepdims=False)
        allowed = (pair_row[key_tile] & key_ok)[None, :]
        masked = jnp.where(allowed, scores, -1e+30)
        row_peak = lax.optimization_barrier(jnp.max(masked, axis=1, keepdims=True))
        weights = jnp.where(allowed, jnp.exp(masked - row_peak), 0.0)
        row_total = lax.optimization_barrier(jnp.sum(weights, axis=1, keepdims=True))
        summed = jnp.dot(weights.astype(jnp.bfloat16), v_head, preferred_element_type=jnp.float32)
        return (summed / row_total).astype(jnp.bfloat16)
    results = lax.map(attend_one, jnp.arange(TILES * H, dtype=jnp.int32))
    attended = results.reshape(TILES, H, TILE, HD).transpose(0, 2, 1, 3).reshape(TOKENS, H * HD)
    groups = N_TP * N_SUB
    group_width = H // groups * HD
    group_inputs = attended.reshape(TOKENS, groups, group_width).transpose(1, 0, 2)
    group_weights = w_out.reshape(groups, group_width, D)

    def add_group(total, pieces):
        inputs_g, weights_g = pieces
        partial_value = jnp.dot(inputs_g, weights_g, preferred_element_type=jnp.float32).astype(jnp.bfloat16)
        partial_value = lax.optimization_barrier(partial_value)
        return (total + partial_value.astype(jnp.float32), None)
    projected, unused = lax.scan(add_group, jnp.zeros((TOKENS, D), jnp.float32), (group_inputs, group_weights))
    return (latents.astype(jnp.float32) + mod_gate * projected).astype(jnp.bfloat16)
```

```python
import functools
import math

import jax
import jax.numpy as jnp
from jax import lax
from jax.experimental import pallas as pl
from jax.experimental.pallas import tpu as pltpu
from jax.sharding import PartitionSpec as P


AXES = ("rep", "seq", "tp", "sub")
EPS = 1e-06
NEG = -1e30
F32 = jnp.float32
BF16 = jnp.bfloat16


def norm_kernel(half_ref, x_ref, shift_ref, scale_ref, out_ref):
    x_float = x_ref[...].astype(F32)
    centre = x_float - jnp.mean(x_float, axis=-1, keepdims=True)
    spread = jnp.mean(centre * centre, axis=-1, keepdims=True)
    scaled = centre * lax.rsqrt(spread + EPS) * (1.0 + scale_ref[...])
    out_ref[...] = (scaled + shift_ref[...]).astype(BF16)


def norm_rows(latents, mod_shift, mod_scale, half):
    rows, width = latents.shape
    steps = 4
    block = rows // 2 // steps
    vector = pl.BlockSpec((1, width), lambda i, half_ref: (0, 0))
    return pl.pallas_call(
        norm_kernel,
        out_shape=jax.ShapeDtypeStruct((rows // 2, width), BF16),
        grid_spec=pltpu.PrefetchScalarGridSpec(
            num_scalar_prefetch=1,
            grid=(steps,),
            in_specs=[
                pl.BlockSpec((block, width), lambda i, half_ref: (half_ref[0] * steps + i, 0)),
                vector,
                vector,
            ],
            out_specs=pl.BlockSpec((block, width), lambda i, half_ref: (i, 0)),
        ),
        compiler_params=pltpu.CompilerParams(vmem_limit_bytes=12 << 20),
        cost_estimate=pl.CostEstimate(flops=rows * width * 5, bytes_accessed=rows * width * 2, transcendentals=rows),
        name="norm_rows",
    )(half[None], latents, mod_shift[None], mod_scale[None])


def head_norm(raw, gain):
    square = jnp.mean(raw * raw, axis=-1, keepdims=True)
    return (raw * lax.rsqrt(square + EPS) * gain).astype(BF16)


def qkv_kernel(sc_ref, ta_ref, tb_ref, *rest):
    w_refs, (gq_ref, gk_ref, q_ref, kv_ref) = rest[:8], rest[8:]
    half_rows = ta_ref.shape[0]
    _, heads, depth, hd = w_refs[0].shape
    first, second = sc_ref[4], 1 - sc_ref[4]
    acc = None
    for b in range(4):
        base = sc_ref[b] * (2 * depth)
        cols = [pl.ds(pl.multiple_of(base + h * depth, 128), depth) for h in (first, second)]
        toks = jnp.concatenate(
            [jnp.concatenate([t_ref[:, cs] for cs in cols], axis=1) for t_ref in (ta_ref, tb_ref)], axis=0
        )
        w = jnp.concatenate(
            [
                jnp.concatenate([w_refs[2 * b + i][s, h] for s in range(3) for h in range(heads)], axis=1)
                for i in range(2)
            ],
            axis=0,
        )
        term = jnp.dot(toks, w, preferred_element_type=F32)
        acc = term if acc is None else acc + term
    col = sc_ref[5]
    for part in range(2):
        where_to = pl.ds(pl.multiple_of((col if part == 0 else 1 - col) * half_rows, 64), half_rows)
        rows = acc[part * half_rows : (part + 1) * half_rows]
        for h in range(heads):
            lanes = slice(h * hd, (h + 1) * hd)
            q_ref[where_to, lanes] = head_norm(rows[:, lanes], gq_ref[...])
            kv_ref[where_to, lanes] = head_norm(rows[:, (heads + h) * hd : (heads + h + 1) * hd], gk_ref[...])
        kv_ref[where_to, heads * hd :] = rows[:, 2 * heads * hd :].astype(BF16)


def qkv_tile(scalars, ta, tb, w_halves, query_gain, key_gain):
    half_rows, width = ta.shape
    _, heads, depth, hd = w_halves[0].shape
    rows = 2 * half_rows
    smem = pl.BlockSpec(memory_space=pltpu.SMEM)
    vmem = pl.BlockSpec(memory_space=pltpu.VMEM)
    return pl.pallas_call(
        qkv_kernel,
        out_shape=(
            jax.ShapeDtypeStruct((rows, heads * hd), BF16),
            jax.ShapeDtypeStruct((rows, 2 * heads * hd), BF16),
        ),
        in_specs=[smem] + [vmem] * 12,
        out_specs=(vmem, vmem),
        compiler_params=pltpu.CompilerParams(vmem_limit_bytes=32 << 20),
        cost_estimate=pl.CostEstimate(
            flops=2 * rows * width * 3 * heads * hd, bytes_accessed=width * 3 * heads * hd * 2, transcendentals=0
        ),
        name="qkv_tile",
    )(scalars, ta, tb, *w_halves, query_gain[None], key_gain[None])


def attend_kernel(sc_ref, qf_ref, qg_ref, kvs0, kvs1, kvs2, kvs3, bias_ref, outf_ref, outg_ref):
    kv_refs = (kvs0, kvs1, kvs2, kvs3)
    rows, width = qf_ref.shape
    hd = 128
    heads = width // hd
    factor = math.log2(math.e) / math.sqrt(hd)
    for t, (q_ref, o_ref) in enumerate(((qf_ref, outf_ref), (qg_ref, outg_ref))):
        bias = jnp.concatenate(
            [
                bias_ref[pl.ds(sc_ref[t], 1), pl.ds(pl.multiple_of(sc_ref[s] * rows, 128), rows)]
                for s in range(4)
            ],
            axis=1,
        )
        for h in range(heads):
            lanes = slice(h * hd, (h + 1) * hd)
            keys = jnp.concatenate([r[:, lanes] for r in kv_refs], axis=0)
            vals = jnp.concatenate([r[:, width + h * hd : width + (h + 1) * hd] for r in kv_refs], axis=0)
            scores = lax.dot_general(
                q_ref[:, lanes], keys, (((1,), (1,)), ((), ())), preferred_element_type=F32
            )
            scores = scores * factor + bias
            weights = jnp.exp2(scores - jnp.max(scores, axis=1, keepdims=True))
            total = jnp.sum(weights, axis=1, keepdims=True)
            added = jnp.dot(weights.astype(BF16), vals, preferred_element_type=F32)
            o_ref[:, lanes] = (added / total).astype(BF16)


def attend(scalars, q_pair, kvs, bias):
    rows, width = q_pair[0].shape
    smem = pl.BlockSpec(memory_space=pltpu.SMEM)
    vmem = pl.BlockSpec(memory_space=pltpu.VMEM)
    shape = jax.ShapeDtypeStruct((rows, width), BF16)
    keys = bias.shape[1]
    return pl.pallas_call(
        attend_kernel,
        out_shape=(shape, shape),
        in_specs=[smem] + [vmem] * 7,
        out_specs=(vmem, vmem),
        compiler_params=pltpu.CompilerParams(vmem_limit_bytes=32 << 20),
        cost_estimate=pl.CostEstimate(
            flops=8 * rows * keys * width, bytes_accessed=8 * rows * width * 2, transcendentals=2 * rows * keys * width // 128
        ),
        name="attend",
    )(scalars, *q_pair, *kvs, bias)


def project_kernel(sc_ref, ne_ref, no_ref, fe_ref, fo_ref, f0, f1, g0, g1, keep_ref, send_ref):
    near = jnp.concatenate([ne_ref[...], no_ref[...]], axis=1)
    far = jnp.concatenate([fe_ref[...], fo_ref[...]], axis=1)
    low = sc_ref[0] == 0
    first, second = jnp.where(low, near, far), jnp.where(low, far, near)

    def block(w0, w1):
        terms = [
            jnp.dot(a, w[...], preferred_element_type=F32).astype(BF16).astype(F32)
            for a, w in ((first, w0), (second, w1))
        ]
        return terms[0] + terms[1]

    @pl.when(sc_ref[1] == 1)
    def _():
        send_ref[...] = block(g0, g1).astype(BF16)
        keep_ref[...] = block(f0, f1)

    @pl.when(sc_ref[1] == 0)
    def _():
        send_ref[...] = block(f0, f1).astype(BF16)
        keep_ref[...] = block(g0, g1)


def project(scalars, pieces, weights):
    rows = pieces[0].shape[0]
    depth, width = weights[0].shape
    smem = pl.BlockSpec(memory_space=pltpu.SMEM)
    vmem = pl.BlockSpec(memory_space=pltpu.VMEM)
    return pl.pallas_call(
        project_kernel,
        out_shape=(jax.ShapeDtypeStruct((rows, width), F32), jax.ShapeDtypeStruct((rows, width), BF16)),
        in_specs=[smem] + [vmem] * 8,
        out_specs=(vmem, vmem),
        compiler_params=pltpu.CompilerParams(vmem_limit_bytes=32 << 20),
        cost_estimate=pl.CostEstimate(
            flops=8 * rows * depth * width, bytes_accessed=4 * depth * width * 2, transcendentals=0
        ),
        name="project",
    )(scalars, *pieces, *weights)


def scalars_of(*values):
    return jnp.stack([jnp.asarray(v, jnp.int32) for v in values])


def line_local(
    sizes,
    latents,
    w_qkv,
    w_out,
    query_gain,
    key_gain,
    mod_shift,
    mod_scale,
    mod_gate,
    block_list,
    block_live,
    key_valid,
):
    ny, nz, nx, nc = sizes
    y, z, x, c = (lax.axis_index(a) for a in AXES)

    def move(array, target):
        pairs = []
        for yy in range(ny):
            for zz in range(nz):
                for xx in range(nx):
                    for cc in range(nc):
                        to = target(yy, zz, xx, cc)
                        if to is not None:
                            flat = lambda p: ((p[0] * nz + p[1]) * nx + p[2]) * nc + p[3]
                            pairs.append((flat((yy, zz, xx, cc)), flat(to)))
        return lax.ppermute(array, AXES, pairs)

    def owns(zz, cc):
        return zz % 2 == cc

    def mid(zz):
        return zz in (1, 2)

    def other_core(yy, zz, xx, cc):
        return (yy, zz, xx, 1 - cc)

    def other_column(yy, zz, xx, cc):
        return (yy, zz, 1 - xx, cc)

    def other_replica(yy, zz, xx, cc):
        return (1 - yy, zz, xx, cc)

    own = z % 2 == c
    is_mid = (z == 1) | (z == 2)
    pair = z // 2
    parity = z % 2

    rows, width = latents.shape
    depth, _, heads_here, hd = w_qkv.shape
    heads = heads_here * nc // nz
    half = depth // 2

    w_t = jnp.transpose(w_qkv, (1, 2, 0, 3))

    def weights_for(slot, which):
        return lax.dynamic_slice(w_t, (0, slot * heads, which * half, 0), (3, heads, half, hd))

    home = pair == c
    slot_a = jnp.where(home, 1 - parity, parity)
    slot_b = jnp.where(home, parity, 1 - parity)
    msg_a = weights_for(slot_a, y)
    msg_b = weights_for(slot_b, y)
    own_rest = weights_for(slot_b, 1 - y)
    z_a = move(
        msg_a, lambda yy, zz, xx, cc: (yy, zz ^ 1, xx, 1) if zz // 2 == cc else (yy, zz ^ 2, xx, 0)
    )

    n_mine = norm_rows(latents, mod_shift, mod_scale, x)
    r1 = move(n_mine, lambda yy, zz, xx, cc: (yy, zz ^ 1, xx, cc) if owns(zz, cc) else None)
    r2a = move(n_mine, lambda yy, zz, xx, cc: (yy, 3 - zz, xx, cc) if owns(zz, cc) and mid(zz) else None)
    z_b = move(msg_b, lambda yy, zz, xx, cc: (yy, zz ^ 3, xx, zz // 2) if zz // 2 != cc else None)
    n_other = norm_rows(latents, mod_shift, mod_scale, 1 - x)

    def pass_on_a(yy, zz, xx, cc):
        return (yy, zz ^ 1, xx, cc) if mid(zz) and not owns(zz, cc) else None

    def pass_on_b(yy, zz, xx, cc):
        return (yy, zz ^ 1, xx, cc) if mid(zz) and owns(zz, cc) else None

    def across_b(yy, zz, xx, cc):
        return (yy, 3 - zz, xx, cc) if mid(zz) and not owns(zz, cc) else None

    def far_of(a2, b2, a3, b3):
        return jnp.where(is_mid, jnp.where(own, b2, a2), jnp.where(own, a3, b3))

    r2b = move(r1, across_b)
    r3a = move(r2a, pass_on_a)
    r3b = move(r2b, pass_on_b)
    x_r1 = move(r1, lambda yy, zz, xx, cc: None if owns(zz, cc) else (yy, zz, 1 - xx, cc))
    far_mine = far_of(r2a, r2b, r3a, r3b)
    far_other = move(far_mine, other_column)
    near_mine = jnp.where(own, n_mine, r1)
    near_other = jnp.where(own, n_other, x_r1)

    y_a = move(z_a, other_replica)
    y_b = move(z_b, lambda yy, zz, xx, cc: (1 - yy, zz, xx, cc) if zz // 2 != cc else None)
    l1 = jnp.where(home, msg_b, z_b)
    l2 = jnp.where(home, own_rest, y_b)
    w_halves = (
        z_a,
        y_a,
        move(z_a, other_core),
        move(y_a, other_core),
        l1,
        l2,
        move(l1, other_core),
        move(l2, other_core),
    )
    near_z, far_z = z ^ 1, z ^ 2
    w_sources = (
        jnp.where(c == 0, far_z, near_z),
        jnp.where(c == 0, near_z, far_z),
        jnp.where(home, z, z ^ 3),
        jnp.where(home, z ^ 3, z),
    )
    qkv_scalars = scalars_of(*w_sources, y, x)

    tile_ids = jnp.arange(nz, dtype=jnp.int32)
    hits = jnp.any((block_list[0][:, None] == tile_ids[None]) & (block_live[0][:, None] > 0), axis=0)
    flags = jnp.concatenate([key_valid, jnp.pad(hits.astype(jnp.int32), (0, 128 - nz))])
    flags = lax.all_gather(flags, "seq", axis=0, tiled=False)
    allowed = (flags[:, rows : rows + nz][:, :, None] > 0) & (flags[None, :, :rows] > 0)
    bias = jnp.where(allowed, 0.0, NEG).astype(F32).reshape(nz, nz * rows)

    q_near, kv_near = qkv_tile(qkv_scalars, near_mine, near_other, w_halves, query_gain, key_gain)
    kv_near_o = move(kv_near, other_core)
    q_far, kv_far = qkv_tile(qkv_scalars, far_mine, far_other, w_halves, query_gain, key_gain)
    kv_far_o = move(kv_far, other_core)

    tiles = scalars_of(
        2 * pair + c, 2 * (1 - pair) + c, 2 * pair + 1 - c, 2 * (1 - pair) + 1 - c
    )
    att_near, att_far = attend(tiles, (q_near, q_far), (kv_near, kv_far, kv_near_o, kv_far_o), bias)

    wo = w_out.reshape(heads_here * hd, w_out.shape[2])
    s1 = move(wo, lambda yy, zz, xx, cc: (yy, zz ^ 1, xx, zz % 2) if cc == yy else None)
    s2a = move(wo, lambda yy, zz, xx, cc: (yy, 3 - zz, xx, zz % 2) if cc == yy and mid(zz) else None)
    c_f = move(wo, lambda yy, zz, xx, cc: None if owns(zz, cc) else (yy, zz, xx, 1 - cc))
    s2b = move(s1, across_b)
    s3a = move(s2a, pass_on_a)
    s3b = move(s2b, pass_on_b)
    y_f = move(s1, lambda yy, zz, xx, cc: None if owns(zz, cc) else (1 - yy, zz, xx, cc))
    g_z = far_of(s2a, s2b, s3a, s3b)
    y_g = move(g_z, other_replica)
    f_first = [
        jnp.where(own, jnp.where(c == g, wo, c_f), jnp.where(y == g, s1, y_f)) for g in range(2)
    ]
    f_second = [jnp.where(y == g, g_z, y_g) for g in range(2)]

    p_near = move(att_near, lambda yy, zz, xx, cc: None if owns(zz, cc) else (yy, zz ^ 1, xx, cc))
    p_far = move(att_far, lambda yy, zz, xx, cc: (yy, 2 * (1 - zz // 2) + cc, xx, zz % 2))
    p_far_o = move(p_far, other_core)
    to_other = lambda yy, zz, xx, cc: (yy, zz, xx, 1 - cc) if owns(zz, cc) else None
    piece_own = jnp.where(own, att_near, move(att_near, to_other))
    piece_pair = jnp.where(own, p_near, move(p_near, to_other))
    even = parity == 0
    pieces = (
        jnp.where(even, piece_own, piece_pair),
        jnp.where(even, piece_pair, piece_own),
        jnp.where(c == 0, p_far, p_far_o),
        jnp.where(c == 0, p_far_o, p_far),
    )

    keep, send = project(scalars_of(pair, x == pair), pieces, (*f_first, *f_second))
    projected = keep + move(send, other_column).astype(F32)
    out_width = projected.shape[1]
    offset = (x * nc + c) * out_width
    latent_cols = lax.dynamic_slice_in_dim(latents, offset, out_width, 1).astype(F32)
    gate_cols = lax.dynamic_slice_in_dim(mod_gate, offset, out_width, 0)
    return (latent_cols + gate_cols * projected).astype(BF16)


def modulate(latents, mod_shift, mod_scale):
    x_float = latents.astype(F32)
    centre = x_float - jnp.mean(x_float, axis=-1, keepdims=True)
    spread = jnp.mean(centre * centre, axis=-1, keepdims=True)
    return (centre * lax.rsqrt(spread + EPS) * (1.0 + mod_scale) + mod_shift).astype(BF16)


def gather_local(
    latents,
    w_qkv,
    w_out,
    query_gain,
    key_gain,
    mod_shift,
    mod_scale,
    mod_gate,
    block_list,
    block_live,
    key_valid,
):
    gather = functools.partial(lax.all_gather, axis_name="seq", tiled=True)
    tok_rows = latents.shape[0]
    tile = tok_rows // block_list.shape[0]
    tiles_all = block_list.shape[0] * lax.axis_size("seq")
    normed = modulate(latents, mod_shift, mod_scale)
    qkv = jnp.einsum("td,dshe->tshe", normed, gather(w_qkv, axis=0), preferred_element_type=F32)
    queries = head_norm(qkv[:, 0], query_gain)
    keys = gather(head_norm(qkv[:, 1], key_gain), axis=0)
    values = gather(qkv[:, 2].astype(BF16), axis=0)
    key_ok = gather(key_valid, axis=0) > 0
    tile_ids = jnp.arange(tiles_all, dtype=jnp.int32)
    hits = jnp.any(
        (block_list[:, :, None] == tile_ids[None, None, :]) & (block_live[:, :, None] > 0), axis=1
    )
    allowed = jnp.repeat(jnp.repeat(hits, tile, axis=0), tile, axis=1) & key_ok[None, :]
    scores = jnp.einsum("qhe,khe->hqk", queries, keys, preferred_element_type=F32) / math.sqrt(
        queries.shape[-1]
    )
    masked = jnp.where(allowed[None], scores, NEG)
    weights = jnp.where(allowed[None], jnp.exp(masked - jnp.max(masked, axis=2, keepdims=True)), 0.0)
    total = jnp.sum(weights, axis=2)
    weighted = jnp.einsum("hqk,khe->qhe", weights.astype(BF16), values, preferred_element_type=F32)
    attended = (weighted / jnp.transpose(total)[:, :, None]).astype(BF16)
    head_terms = jnp.einsum("the,hec->tc", attended, gather(w_out, axis=2), preferred_element_type=F32)
    projected = lax.psum_scatter(
        head_terms.astype(BF16), ("tp", "sub"), scatter_dimension=1, tiled=True
    ).astype(F32)
    out_width = projected.shape[1]
    offset = lax.axis_index(("tp", "sub")) * out_width
    latent_cols = lax.dynamic_slice_in_dim(latents, offset, out_width, 1).astype(F32)
    gate_cols = lax.dynamic_slice_in_dim(mod_gate, offset, out_width, 0)
    return (latent_cols + gate_cols * projected).astype(BF16)


def solution(mesh):
    sizes = tuple(mesh.shape[a] for a in AXES)

    def local(*args):
        ny, nz, nx, nc = sizes
        heads_here, block_list = args[1].shape[2], args[8]
        line = ny == nx == nc == 2 and nz == nc * 2 and heads_here % nc == 0 and block_list.shape[0] == 1
        if line:
            return line_local(sizes, *args)
        return gather_local(*args)

    in_specs = (
        P(("rep", "seq"), None),
        P("seq", None, ("tp", "sub"), None),
        P(("tp", "sub"), None, "seq"),
        P(),
        P(),
        P("rep"),
        P("rep"),
        P("rep"),
        P(("rep", "seq"), None),
        P(("rep", "seq"), None),
        P(("rep", "seq")),
    )
    out_specs = P(("rep", "seq"), ("tp", "sub"))
    return jax.shard_map(local, mesh=mesh, in_specs=in_specs, out_specs=out_specs, check_vma=False)
```

```python
import functools
import math

import jax
import jax.numpy as jnp
from jax import lax
from jax.experimental import pallas as pl
from jax.experimental.pallas import tpu as pltpu
from jax.sharding import PartitionSpec as P


AXES = ("rep", "seq", "tp", "sub")
EPS = 1e-06
NEG = -1e30
F32 = jnp.float32
BF16 = jnp.bfloat16


def norm_kernel(half_ref, x_ref, shift_ref, scale_ref, out_ref):
    x_float = x_ref[...].astype(F32)
    centre = x_float - jnp.mean(x_float, axis=-1, keepdims=True)
    spread = jnp.mean(centre * centre, axis=-1, keepdims=True)
    scaled = centre * lax.rsqrt(spread + EPS) * (1.0 + scale_ref[...])
    out_ref[...] = (scaled + shift_ref[...]).astype(BF16)


def norm_rows(latents, mod_shift, mod_scale, half):
    rows, width = latents.shape
    steps = 4
    block = rows // 2 // steps
    vector = pl.BlockSpec((1, width), lambda i, half_ref: (0, 0))
    return pl.pallas_call(
        norm_kernel,
        out_shape=jax.ShapeDtypeStruct((rows // 2, width), BF16),
        grid_spec=pltpu.PrefetchScalarGridSpec(
            num_scalar_prefetch=1,
            grid=(steps,),
            in_specs=[
                pl.BlockSpec((block, width), lambda i, half_ref: (half_ref[0] * steps + i, 0)),
                vector,
                vector,
            ],
            out_specs=pl.BlockSpec((block, width), lambda i, half_ref: (i, 0)),
        ),
        compiler_params=pltpu.CompilerParams(vmem_limit_bytes=12 << 20),
        cost_estimate=pl.CostEstimate(flops=rows * width * 5, bytes_accessed=rows * width * 2, transcendentals=rows),
        name="norm_rows",
    )(half[None], latents, mod_shift[None], mod_scale[None])


def head_norm(raw, gain):
    square = jnp.mean(raw * raw, axis=-1, keepdims=True)
    return (raw * lax.rsqrt(square + EPS) * gain).astype(BF16)


def qkv_kernel(sc_ref, ta_ref, tb_ref, *rest):
    w_refs, (gq_ref, gk_ref, q_ref, kv_ref) = rest[:8], rest[8:]
    half_rows = ta_ref.shape[0]
    _, heads, depth, hd = w_refs[0].shape
    first, second = sc_ref[4], 1 - sc_ref[4]
    acc = None
    for b in range(4):
        base = sc_ref[b] * (2 * depth)
        cols = [pl.ds(pl.multiple_of(base + h * depth, 128), depth) for h in (first, second)]
        toks = jnp.concatenate(
            [jnp.concatenate([t_ref[:, cs] for cs in cols], axis=1) for t_ref in (ta_ref, tb_ref)], axis=0
        )
        w = jnp.concatenate(
            [
                jnp.concatenate([w_refs[2 * b + i][s, h] for s in range(3) for h in range(heads)], axis=1)
                for i in range(2)
            ],
            axis=0,
        )
        term = jnp.dot(toks, w, preferred_element_type=F32)
        acc = term if acc is None else acc + term
    col = sc_ref[5]
    for part in range(2):
        where_to = pl.ds(pl.multiple_of((col if part == 0 else 1 - col) * half_rows, 64), half_rows)
        rows = acc[part * half_rows : (part + 1) * half_rows]
        for h in range(heads):
            lanes = slice(h * hd, (h + 1) * hd)
            q_ref[where_to, lanes] = head_norm(rows[:, lanes], gq_ref[...])
            kv_ref[where_to, lanes] = head_norm(rows[:, (heads + h) * hd : (heads + h + 1) * hd], gk_ref[...])
        kv_ref[where_to, heads * hd :] = rows[:, 2 * heads * hd :].astype(BF16)


def qkv_tile(scalars, ta, tb, w_halves, query_gain, key_gain):
    half_rows, width = ta.shape
    _, heads, depth, hd = w_halves[0].shape
    rows = 2 * half_rows
    smem = pl.BlockSpec(memory_space=pltpu.SMEM)
    vmem = pl.BlockSpec(memory_space=pltpu.VMEM)
    return pl.pallas_call(
        qkv_kernel,
        out_shape=(
            jax.ShapeDtypeStruct((rows, heads * hd), BF16),
            jax.ShapeDtypeStruct((rows, 2 * heads * hd), BF16),
        ),
        in_specs=[smem] + [vmem] * 12,
        out_specs=(vmem, vmem),
        compiler_params=pltpu.CompilerParams(vmem_limit_bytes=32 << 20),
        cost_estimate=pl.CostEstimate(
            flops=2 * rows * width * 3 * heads * hd, bytes_accessed=width * 3 * heads * hd * 2, transcendentals=0
        ),
        name="qkv_tile",
    )(scalars, ta, tb, *w_halves, query_gain[None], key_gain[None])


def attend_kernel(sc_ref, qf_ref, qg_ref, kvs0, kvs1, kvs2, kvs3, bias_ref, outf_ref, outg_ref):
    kv_refs = (kvs0, kvs1, kvs2, kvs3)
    rows, width = qf_ref.shape
    hd = 128
    heads = width // hd
    factor = math.log2(math.e) / math.sqrt(hd)
    for t, (q_ref, o_ref) in enumerate(((qf_ref, outf_ref), (qg_ref, outg_ref))):
        bias = jnp.concatenate(
            [
                bias_ref[pl.ds(sc_ref[t], 1), pl.ds(pl.multiple_of(sc_ref[s] * rows, 128), rows)]
                for s in range(4)
            ],
            axis=1,
        )
        for h in range(heads):
            lanes = slice(h * hd, (h + 1) * hd)
            keys = jnp.concatenate([r[:, lanes] for r in kv_refs], axis=0)
            vals = jnp.concatenate([r[:, width + h * hd : width + (h + 1) * hd] for r in kv_refs], axis=0)
            scores = lax.dot_general(
                q_ref[:, lanes], keys, (((1,), (1,)), ((), ())), preferred_element_type=F32
            )
            scores = scores * factor + bias
            weights = jnp.exp2(scores - jnp.max(scores, axis=1, keepdims=True))
            total = jnp.sum(weights, axis=1, keepdims=True)
            added = jnp.dot(weights.astype(BF16), vals, preferred_element_type=F32)
            o_ref[:, lanes] = (added / total).astype(BF16)


def attend(scalars, q_pair, kvs, bias):
    rows, width = q_pair[0].shape
    smem = pl.BlockSpec(memory_space=pltpu.SMEM)
    vmem = pl.BlockSpec(memory_space=pltpu.VMEM)
    shape = jax.ShapeDtypeStruct((rows, width), BF16)
    keys = bias.shape[1]
    return pl.pallas_call(
        attend_kernel,
        out_shape=(shape, shape),
        in_specs=[smem] + [vmem] * 7,
        out_specs=(vmem, vmem),
        compiler_params=pltpu.CompilerParams(vmem_limit_bytes=32 << 20),
        cost_estimate=pl.CostEstimate(
            flops=8 * rows * keys * width, bytes_accessed=8 * rows * width * 2, transcendentals=2 * rows * keys * width // 128
        ),
        name="attend",
    )(scalars, *q_pair, *kvs, bias)


def project_kernel(sc_ref, ne_ref, no_ref, fe_ref, fo_ref, f0, f1, g0, g1, out_ref):
    near = jnp.concatenate([ne_ref[...], no_ref[...]], axis=1)
    far = jnp.concatenate([fe_ref[...], fo_ref[...]], axis=1)
    low = sc_ref[0] == 0
    first, second = jnp.where(low, near, far), jnp.where(low, far, near)

    def block(w0, w1):
        terms = [
            jnp.dot(a, w[...], preferred_element_type=F32).astype(BF16).astype(F32)
            for a, w in ((first, w0), (second, w1))
        ]
        return terms[0] + terms[1]

    @pl.when(sc_ref[1] == 0)
    def _():
        out_ref[...] = block(f0, f1).astype(out_ref.dtype)

    @pl.when(sc_ref[1] == 1)
    def _():
        out_ref[...] = block(g0, g1).astype(out_ref.dtype)


def project(scalars, pieces, weights, dtype):
    rows = pieces[0].shape[0]
    depth, width = weights[0].shape
    smem = pl.BlockSpec(memory_space=pltpu.SMEM)
    vmem = pl.BlockSpec(memory_space=pltpu.VMEM)
    return pl.pallas_call(
        project_kernel,
        out_shape=jax.ShapeDtypeStruct((rows, width), dtype),
        in_specs=[smem] + [vmem] * 8,
        out_specs=vmem,
        compiler_params=pltpu.CompilerParams(vmem_limit_bytes=32 << 20),
        cost_estimate=pl.CostEstimate(
            flops=4 * rows * depth * width, bytes_accessed=4 * depth * width * 2, transcendentals=0
        ),
        name="project",
    )(scalars, *pieces, *weights)


def scalars_of(*values):
    return jnp.stack([jnp.asarray(v, jnp.int32) for v in values])


def line_local(
    sizes,
    latents,
    w_qkv,
    w_out,
    query_gain,
    key_gain,
    mod_shift,
    mod_scale,
    mod_gate,
    block_list,
    block_live,
    key_valid,
):
    ny, nz, nx, nc = sizes
    y, z, x, c = (lax.axis_index(a) for a in AXES)

    def move(array, target):
        pairs = []
        for yy in range(ny):
            for zz in range(nz):
                for xx in range(nx):
                    for cc in range(nc):
                        to = target(yy, zz, xx, cc)
                        if to is not None:
                            flat = lambda p: ((p[0] * nz + p[1]) * nx + p[2]) * nc + p[3]
                            pairs.append((flat((yy, zz, xx, cc)), flat(to)))
        return lax.ppermute(array, AXES, pairs)

    def owns(zz, cc):
        return zz % 2 == cc

    def mid(zz):
        return zz in (1, 2)

    def other_core(yy, zz, xx, cc):
        return (yy, zz, xx, 1 - cc)

    def other_column(yy, zz, xx, cc):
        return (yy, zz, 1 - xx, cc)

    def other_replica(yy, zz, xx, cc):
        return (1 - yy, zz, xx, cc)

    own = z % 2 == c
    is_mid = (z == 1) | (z == 2)
    pair = z // 2
    parity = z % 2

    rows, width = latents.shape
    depth, _, heads_here, hd = w_qkv.shape
    heads = heads_here * nc // nz
    half = depth // 2

    w_t = jnp.transpose(w_qkv, (1, 2, 0, 3))

    def weights_for(slot, which):
        return lax.dynamic_slice(w_t, (0, slot * heads, which * half, 0), (3, heads, half, hd))

    home = pair == c
    slot_a = jnp.where(home, 1 - parity, parity)
    slot_b = jnp.where(home, parity, 1 - parity)
    msg_a = weights_for(slot_a, y)
    msg_b = weights_for(slot_b, y)
    own_rest = weights_for(slot_b, 1 - y)
    z_a = move(
        msg_a, lambda yy, zz, xx, cc: (yy, zz ^ 1, xx, 1) if zz // 2 == cc else (yy, zz ^ 2, xx, 0)
    )

    n_mine = norm_rows(latents, mod_shift, mod_scale, x)
    r1 = move(n_mine, lambda yy, zz, xx, cc: (yy, zz ^ 1, xx, cc) if owns(zz, cc) else None)
    r2a = move(n_mine, lambda yy, zz, xx, cc: (yy, 3 - zz, xx, cc) if owns(zz, cc) and mid(zz) else None)
    z_b = move(msg_b, lambda yy, zz, xx, cc: (yy, zz ^ 3, xx, zz // 2) if zz // 2 != cc else None)
    n_other = norm_rows(latents, mod_shift, mod_scale, 1 - x)

    def pass_on_a(yy, zz, xx, cc):
        return (yy, zz ^ 1, xx, cc) if mid(zz) and not owns(zz, cc) else None

    def pass_on_b(yy, zz, xx, cc):
        return (yy, zz ^ 1, xx, cc) if mid(zz) and owns(zz, cc) else None

    def across_b(yy, zz, xx, cc):
        return (yy, 3 - zz, xx, cc) if mid(zz) and not owns(zz, cc) else None

    def far_of(a2, b2, a3, b3):
        return jnp.where(is_mid, jnp.where(own, b2, a2), jnp.where(own, a3, b3))

    r2b = move(r1, across_b)
    r3a = move(r2a, pass_on_a)
    r3b = move(r2b, pass_on_b)
    x_r1 = move(r1, lambda yy, zz, xx, cc: None if owns(zz, cc) else (yy, zz, 1 - xx, cc))
    far_mine = far_of(r2a, r2b, r3a, r3b)
    far_other = move(far_mine, other_column)
    near_mine = jnp.where(own, n_mine, r1)
    near_other = jnp.where(own, n_other, x_r1)

    y_a = move(z_a, other_replica)
    y_b = move(z_b, lambda yy, zz, xx, cc: (1 - yy, zz, xx, cc) if zz // 2 != cc else None)
    l1 = jnp.where(home, msg_b, z_b)
    l2 = jnp.where(home, own_rest, y_b)
    w_halves = (
        z_a,
        y_a,
        move(z_a, other_core),
        move(y_a, other_core),
        l1,
        l2,
        move(l1, other_core),
        move(l2, other_core),
    )
    near_z, far_z = z ^ 1, z ^ 2
    w_sources = (
        jnp.where(c == 0, far_z, near_z),
        jnp.where(c == 0, near_z, far_z),
        jnp.where(home, z, z ^ 3),
        jnp.where(home, z ^ 3, z),
    )
    qkv_scalars = scalars_of(*w_sources, y, x)

    tile_ids = jnp.arange(nz, dtype=jnp.int32)
    hits = jnp.any((block_list[0][:, None] == tile_ids[None]) & (block_live[0][:, None] > 0), axis=0)
    flags = jnp.concatenate([key_valid, jnp.pad(hits.astype(jnp.int32), (0, 128 - nz))])[None]
    by_step = [flags] + [move(flags, lambda yy, zz, xx, cc, d=d: (yy, zz ^ d, xx, cc)) for d in range(1, nz)]
    flags = jnp.concatenate(
        [functools.reduce(lambda a, d: jnp.where(z ^ d == t, by_step[d], a), range(nz), flags) for t in range(nz)]
    )
    allowed = (flags[:, rows : rows + nz][:, :, None] > 0) & (flags[None, :, :rows] > 0)
    bias = jnp.where(allowed, 0.0, NEG).astype(F32).reshape(nz, nz * rows)

    q_near, kv_near = qkv_tile(qkv_scalars, near_mine, near_other, w_halves, query_gain, key_gain)
    kv_near_o = move(kv_near, other_core)
    q_far, kv_far = qkv_tile(qkv_scalars, far_mine, far_other, w_halves, query_gain, key_gain)
    kv_far_o = move(kv_far, other_core)

    tiles = scalars_of(
        2 * pair + c, 2 * (1 - pair) + c, 2 * pair + 1 - c, 2 * (1 - pair) + 1 - c
    )
    att_near, att_far = attend(tiles, (q_near, q_far), (kv_near, kv_far, kv_near_o, kv_far_o), bias)

    wo = w_out.reshape(heads_here * hd, w_out.shape[2])
    s1 = move(wo, lambda yy, zz, xx, cc: (yy, zz ^ 1, xx, zz % 2) if cc == yy else None)
    s2a = move(wo, lambda yy, zz, xx, cc: (yy, 3 - zz, xx, zz % 2) if cc == yy and mid(zz) else None)
    c_f = move(wo, lambda yy, zz, xx, cc: None if owns(zz, cc) else (yy, zz, xx, 1 - cc))
    s2b = move(s1, across_b)
    s3a = move(s2a, pass_on_a)
    s3b = move(s2b, pass_on_b)
    y_f = move(s1, lambda yy, zz, xx, cc: None if owns(zz, cc) else (1 - yy, zz, xx, cc))
    g_z = far_of(s2a, s2b, s3a, s3b)
    y_g = move(g_z, other_replica)
    f_first = [
        jnp.where(own, jnp.where(c == g, wo, c_f), jnp.where(y == g, s1, y_f)) for g in range(2)
    ]
    f_second = [jnp.where(y == g, g_z, y_g) for g in range(2)]

    p_near = move(att_near, lambda yy, zz, xx, cc: None if owns(zz, cc) else (yy, zz ^ 1, xx, cc))
    p_far = move(att_far, lambda yy, zz, xx, cc: (yy, 2 * (1 - zz // 2) + cc, xx, zz % 2))
    p_far_o = move(p_far, other_core)
    to_other = lambda yy, zz, xx, cc: (yy, zz, xx, 1 - cc) if owns(zz, cc) else None
    piece_own = jnp.where(own, att_near, move(att_near, to_other))
    piece_pair = jnp.where(own, p_near, move(p_near, to_other))
    even = parity == 0
    pieces = (
        jnp.where(even, piece_own, piece_pair),
        jnp.where(even, piece_pair, piece_own),
        jnp.where(c == 0, p_far, p_far_o),
        jnp.where(c == 0, p_far_o, p_far),
    )

    blocks = (*f_first, *f_second)
    send = project(scalars_of(pair, x == pair), pieces, blocks, BF16)
    got = move(send, other_column)
    keep = project(scalars_of(pair, x != pair), pieces, blocks, F32)
    projected = keep + got.astype(F32)
    out_width = projected.shape[1]
    offset = (x * nc + c) * out_width
    latent_cols = lax.dynamic_slice_in_dim(latents, offset, out_width, 1).astype(F32)
    gate_cols = lax.dynamic_slice_in_dim(mod_gate, offset, out_width, 0)
    return (latent_cols + gate_cols * projected).astype(BF16)


def modulate(latents, mod_shift, mod_scale):
    x_float = latents.astype(F32)
    centre = x_float - jnp.mean(x_float, axis=-1, keepdims=True)
    spread = jnp.mean(centre * centre, axis=-1, keepdims=True)
    return (centre * lax.rsqrt(spread + EPS) * (1.0 + mod_scale) + mod_shift).astype(BF16)


def gather_local(
    latents,
    w_qkv,
    w_out,
    query_gain,
    key_gain,
    mod_shift,
    mod_scale,
    mod_gate,
    block_list,
    block_live,
    key_valid,
):
    gather = functools.partial(lax.all_gather, axis_name="seq", tiled=True)
    tok_rows = latents.shape[0]
    tile = tok_rows // block_list.shape[0]
    tiles_all = block_list.shape[0] * lax.axis_size("seq")
    normed = modulate(latents, mod_shift, mod_scale)
    qkv = jnp.einsum("td,dshe->tshe", normed, gather(w_qkv, axis=0), preferred_element_type=F32)
    queries = head_norm(qkv[:, 0], query_gain)
    keys = gather(head_norm(qkv[:, 1], key_gain), axis=0)
    values = gather(qkv[:, 2].astype(BF16), axis=0)
    key_ok = gather(key_valid, axis=0) > 0
    tile_ids = jnp.arange(tiles_all, dtype=jnp.int32)
    hits = jnp.any(
        (block_list[:, :, None] == tile_ids[None, None, :]) & (block_live[:, :, None] > 0), axis=1
    )
    allowed = jnp.repeat(jnp.repeat(hits, tile, axis=0), tile, axis=1) & key_ok[None, :]
    scores = jnp.einsum("qhe,khe->hqk", queries, keys, preferred_element_type=F32) / math.sqrt(
        queries.shape[-1]
    )
    masked = jnp.where(allowed[None], scores, NEG)
    weights = jnp.where(allowed[None], jnp.exp(masked - jnp.max(masked, axis=2, keepdims=True)), 0.0)
    total = jnp.sum(weights, axis=2)
    weighted = jnp.einsum("hqk,khe->qhe", weights.astype(BF16), values, preferred_element_type=F32)
    attended = (weighted / jnp.transpose(total)[:, :, None]).astype(BF16)
    head_terms = jnp.einsum("the,hec->tc", attended, gather(w_out, axis=2), preferred_element_type=F32)
    projected = lax.psum_scatter(
        head_terms.astype(BF16), ("tp", "sub"), scatter_dimension=1, tiled=True
    ).astype(F32)
    out_width = projected.shape[1]
    offset = lax.axis_index(("tp", "sub")) * out_width
    latent_cols = lax.dynamic_slice_in_dim(latents, offset, out_width, 1).astype(F32)
    gate_cols = lax.dynamic_slice_in_dim(mod_gate, offset, out_width, 0)
    return (latent_cols + gate_cols * projected).astype(BF16)


def solution(mesh):
    sizes = tuple(mesh.shape[a] for a in AXES)

    def local(*args):
        ny, nz, nx, nc = sizes
        heads_here, block_list = args[1].shape[2], args[8]
        line = ny == nx == nc == 2 and nz == nc * 2 and heads_here % nc == 0 and block_list.shape[0] == 1
        if line:
            return line_local(sizes, *args)
        return gather_local(*args)

    in_specs = (
        P(("rep", "seq"), None),
        P("seq", None, ("tp", "sub"), None),
        P(("tp", "sub"), None, "seq"),
        P(),
        P(),
        P("rep"),
        P("rep"),
        P("rep"),
        P(("rep", "seq"), None),
        P(("rep", "seq"), None),
        P(("rep", "seq")),
    )
    out_specs = P(("rep", "seq"), ("tp", "sub"))
    return jax.shard_map(local, mesh=mesh, in_specs=in_specs, out_specs=out_specs, check_vma=False)
```

```python
import functools
import math

import jax
import jax.numpy as jnp
from jax import lax
from jax.experimental import pallas as pl
from jax.experimental.pallas import tpu as pltpu
from jax.sharding import PartitionSpec as P


AXES = ("rep", "seq", "tp", "sub")
EPS = 1e-06
NEG = -1e30
F32 = jnp.float32
BF16 = jnp.bfloat16


def norm_kernel(half_ref, x_ref, shift_ref, scale_ref, out_ref):
    x_float = x_ref[...].astype(F32)
    centre = x_float - jnp.mean(x_float, axis=-1, keepdims=True)
    spread = jnp.mean(centre * centre, axis=-1, keepdims=True)
    scaled = centre * lax.rsqrt(spread + EPS) * (1.0 + scale_ref[...])
    out_ref[...] = (scaled + shift_ref[...]).astype(BF16)


def norm_rows(latents, mod_shift, mod_scale, half):
    rows, width = latents.shape
    steps = 4
    block = rows // 2 // steps
    vector = pl.BlockSpec((1, width), lambda i, half_ref: (0, 0))
    return pl.pallas_call(
        norm_kernel,
        out_shape=jax.ShapeDtypeStruct((rows // 2, width), BF16),
        grid_spec=pltpu.PrefetchScalarGridSpec(
            num_scalar_prefetch=1,
            grid=(steps,),
            in_specs=[
                pl.BlockSpec((block, width), lambda i, half_ref: (half_ref[0] * steps + i, 0)),
                vector,
                vector,
            ],
            out_specs=pl.BlockSpec((block, width), lambda i, half_ref: (i, 0)),
        ),
        compiler_params=pltpu.CompilerParams(vmem_limit_bytes=12 << 20),
        cost_estimate=pl.CostEstimate(flops=rows * width * 5, bytes_accessed=rows * width * 2, transcendentals=rows),
        name="norm_rows",
    )(half[None], latents, mod_shift[None], mod_scale[None])


def head_norm(raw, gain):
    square = jnp.mean(raw * raw, axis=-1, keepdims=True)
    return (raw * lax.rsqrt(square + EPS) * gain).astype(BF16)


def qkv_kernel(count, sc_ref, *refs):
    mine, others = refs[:count], refs[count : 2 * count]
    za, ya, ca1, ca2, own_w, own_c, zb, yb, cb1, cb2, gq_ref, gk_ref = refs[2 * count : 2 * count + 12]
    q_ref, kv_ref, tok_ref, acc_ref = refs[2 * count + 12 :]
    half_rows = mine[0].shape[0]
    _, heads, depth, hd = za.shape
    col = sc_ref[5]
    for i in range(count):

        @pl.when(sc_ref[7] == i)
        def _():
            tok_ref[pl.ds(pl.multiple_of(col * half_rows, 64), half_rows), :] = mine[i][...]
            tok_ref[pl.ds(pl.multiple_of((1 - col) * half_rows, 64), half_rows), :] = others[i][...]

    def lanes_of(ref, rows):
        return jnp.concatenate([ref[s, h, rows, :] for s in range(3) for h in range(heads)], axis=1)

    def add(block, halves, fresh=False):
        base = sc_ref[block] * (2 * depth)
        if len(halves) == 2:
            cols = [
                tok_ref[:, pl.ds(pl.multiple_of(base + h * depth, 128), depth)] for h in (sc_ref[4], 1 - sc_ref[4])
            ]
            toks = jnp.concatenate(cols, axis=1)
            w = jnp.concatenate([lanes_of(r, slice(None)) for r in halves], axis=0)
        else:
            toks = tok_ref[:, pl.ds(pl.multiple_of(base, 128), 2 * depth)]
            w = lanes_of(halves[0], slice(None))
        term = jnp.dot(toks, w, preferred_element_type=F32)
        acc_ref[...] = term if fresh else acc_ref[...] + term

    add(0, (za, ya), fresh=True)
    add(1, (ca1, ca2))

    @pl.when(sc_ref[6] == 1)
    def _():
        add(2, (own_w,))
        add(3, (cb1, cb2))

    @pl.when(sc_ref[6] == 0)
    def _():
        add(2, (own_c,))
        add(3, (zb, yb))

    for h in range(heads):
        lanes = slice(h * hd, (h + 1) * hd)
        q_ref[:, lanes] = head_norm(acc_ref[:, lanes], gq_ref[...])
        kv_ref[:, lanes] = head_norm(acc_ref[:, (heads + h) * hd : (heads + h + 1) * hd], gk_ref[...])
    kv_ref[:, heads * hd :] = acc_ref[:, 2 * heads * hd :].astype(BF16)


def qkv_tile(scalars, mine, others, weights, query_gain, key_gain):
    half_rows, width = mine[0].shape
    _, heads, _, hd = weights[0].shape
    rows, out = 2 * half_rows, heads * hd
    smem = pl.BlockSpec(memory_space=pltpu.SMEM)
    vmem = pl.BlockSpec(memory_space=pltpu.VMEM)
    return pl.pallas_call(
        functools.partial(qkv_kernel, len(mine)),
        out_shape=(
            jax.ShapeDtypeStruct((rows, out), BF16),
            jax.ShapeDtypeStruct((rows, 2 * out), BF16),
        ),
        in_specs=[smem] + [vmem] * (2 * len(mine) + len(weights) + 2),
        out_specs=(vmem, vmem),
        scratch_shapes=[pltpu.VMEM((rows, width), BF16), pltpu.VMEM((rows, 3 * out), F32)],
        compiler_params=pltpu.CompilerParams(vmem_limit_bytes=32 << 20),
        cost_estimate=pl.CostEstimate(
            flops=6 * rows * width * out, bytes_accessed=width * 3 * out * 2, transcendentals=0
        ),
        name="qkv_tile",
    )(scalars, *mine, *others, *weights, query_gain[None], key_gain[None])


def attend_kernel(sc_ref, q_ref, kvs0, kvs1, kvs2, kvs3, flags_ref, out_ref):
    kv_refs = (kvs0, kvs1, kvs2, kvs3)
    rows, width = q_ref.shape
    hd = 128
    heads = width // hd
    factor = math.log2(math.e) / math.sqrt(hd)
    flags = flags_ref[...]
    place = lax.broadcasted_iota(jnp.int32, flags.shape, 0)

    def row(d):
        return jnp.sum(jnp.where(place == d, flags, 0), axis=0, keepdims=True)

    hits = row(sc_ref[8])[:, rows:]
    lane = lax.broadcasted_iota(jnp.int32, hits.shape, 1)
    biases = []
    for s in range(4):
        hit = jnp.sum(jnp.where(lane == sc_ref[s], hits, 0), axis=1, keepdims=True)
        valid = row(sc_ref[4 + s])[:, :rows]
        biases.append(jnp.where(valid * hit > 0, 0.0, NEG).astype(F32))
    bias = jnp.concatenate(biases, axis=1)
    for h in range(heads):
        lanes = slice(h * hd, (h + 1) * hd)
        keys = jnp.concatenate([r[:, lanes] for r in kv_refs], axis=0)
        vals = jnp.concatenate([r[:, width + h * hd : width + (h + 1) * hd] for r in kv_refs], axis=0)
        scores = lax.dot_general(
            q_ref[:, lanes], keys, (((1,), (1,)), ((), ())), preferred_element_type=F32
        )
        scores = scores * factor + bias
        weights = jnp.exp2(scores - jnp.max(scores, axis=1, keepdims=True))
        total = jnp.sum(weights, axis=1, keepdims=True)
        added = jnp.dot(weights.astype(BF16), vals, preferred_element_type=F32)
        out_ref[:, lanes] = (added / total).astype(BF16)


def attend(scalars, queries, kvs, flags):
    rows, width = queries.shape
    smem = pl.BlockSpec(memory_space=pltpu.SMEM)
    vmem = pl.BlockSpec(memory_space=pltpu.VMEM)
    keys = 4 * rows
    return pl.pallas_call(
        attend_kernel,
        out_shape=jax.ShapeDtypeStruct((rows, width), BF16),
        in_specs=[smem] + [vmem] * 6,
        out_specs=vmem,
        compiler_params=pltpu.CompilerParams(vmem_limit_bytes=32 << 20),
        cost_estimate=pl.CostEstimate(
            flops=4 * rows * keys * width, bytes_accessed=8 * rows * width * 2, transcendentals=rows * keys * width // 128
        ),
        name="attend",
    )(scalars, queries, *kvs, flags)


def project_kernel(sc_ref, an, bn, ap, bp, f0, f1, wo, c_f, s1, y_f, g_z, y_g, out_ref, att_ref):
    _, width = an.shape
    depth = wo.shape[0]

    def put(place, piece_ref):
        att_ref[:, pl.ds(pl.multiple_of(place * width, 128), width)] = piece_ref[...]

    @pl.when(sc_ref[0] == 1)
    def _():
        put(sc_ref[3], an)
        put(sc_ref[4], ap)

    @pl.when(sc_ref[0] == 0)
    def _():
        put(sc_ref[3], bn)
        put(sc_ref[4], bp)

    put(sc_ref[5], f0)
    put(sc_ref[6], f1)

    def term(group, w_ref):
        part = att_ref[:, pl.ds(pl.multiple_of(group * depth, 128), depth)]
        return jnp.dot(part, w_ref[...], preferred_element_type=F32).astype(BF16).astype(F32)

    def block(group, first, second):
        out_ref[...] = (term(group, first) + term(1 - group, second)).astype(out_ref.dtype)

    @pl.when((sc_ref[7] == 1) & (sc_ref[0] == 1))
    def _():
        block(sc_ref[1], wo, c_f)

    @pl.when((sc_ref[7] == 1) & (sc_ref[0] == 0))
    def _():
        block(sc_ref[2], s1, y_f)

    @pl.when(sc_ref[7] == 0)
    def _():
        block(sc_ref[2], g_z, y_g)


def project(scalars, pieces, weights, dtype):
    rows, _ = pieces[0].shape
    depth, width = weights[0].shape
    smem = pl.BlockSpec(memory_space=pltpu.SMEM)
    vmem = pl.BlockSpec(memory_space=pltpu.VMEM)
    return pl.pallas_call(
        project_kernel,
        out_shape=jax.ShapeDtypeStruct((rows, width), dtype),
        in_specs=[smem] + [vmem] * (len(pieces) + len(weights)),
        out_specs=vmem,
        scratch_shapes=[pltpu.VMEM((rows, 2 * depth), BF16)],
        compiler_params=pltpu.CompilerParams(vmem_limit_bytes=16 << 20),
        cost_estimate=pl.CostEstimate(
            flops=4 * rows * depth * width, bytes_accessed=4 * depth * width * 2, transcendentals=0
        ),
        name="project",
    )(scalars, *pieces, *weights)


def scalars_of(*values):
    return jnp.stack([jnp.asarray(v, jnp.int32) for v in values])


def line_local(
    sizes,
    latents,
    w_qkv,
    w_out,
    query_gain,
    key_gain,
    mod_shift,
    mod_scale,
    mod_gate,
    block_list,
    block_live,
    key_valid,
):
    ny, nz, nx, nc = sizes
    y, z, x, c = (lax.axis_index(a) for a in AXES)

    def move(array, target):
        pairs = []
        for yy in range(ny):
            for zz in range(nz):
                for xx in range(nx):
                    for cc in range(nc):
                        to = target(yy, zz, xx, cc)
                        if to is not None:
                            flat = lambda p: ((p[0] * nz + p[1]) * nx + p[2]) * nc + p[3]
                            pairs.append((flat((yy, zz, xx, cc)), flat(to)))
        return lax.ppermute(array, AXES, pairs)

    def owns(zz, cc):
        return zz % 2 == cc

    def home(zz, cc):
        return zz // 2 == cc

    def mid(zz):
        return zz in (1, 2)

    def to_core(who=lambda zz, cc: True):
        return lambda yy, zz, xx, cc: (yy, zz, xx, 1 - cc) if who(zz, cc) else None

    def to_column(who=lambda zz, cc: True):
        return lambda yy, zz, xx, cc: (yy, zz, 1 - xx, cc) if who(zz, cc) else None

    def to_replica(who=lambda zz, cc: True):
        return lambda yy, zz, xx, cc: (1 - yy, zz, xx, cc) if who(zz, cc) else None

    own = z % 2 == c
    at_home = z // 2 == c
    is_mid = (z == 1) | (z == 2)
    pair = z // 2
    parity = z % 2
    near, far = 2 * pair + c, 2 * (1 - pair) + c
    near_o, far_o = 2 * pair + 1 - c, 2 * (1 - pair) + 1 - c

    depth, _, heads_here, hd = w_qkv.shape
    heads = heads_here * nc // nz
    half = depth // 2
    w_t = jnp.transpose(w_qkv, (1, 2, 0, 3))
    wo = w_out.reshape(heads_here * hd, w_out.shape[2])

    def mid_own(zz, cc):
        return mid(zz) and owns(zz, cc)

    def mid_rest(zz, cc):
        return mid(zz) and not owns(zz, cc)

    def end_own(zz, cc):
        return not mid(zz) and owns(zz, cc)

    def end_rest(zz, cc):
        return not mid(zz) and not owns(zz, cc)

    def across(who):
        return lambda yy, zz, xx, cc: (yy, 3 - zz, xx, cc) if who(zz, cc) else None

    def outward(who):
        return lambda yy, zz, xx, cc: (yy, zz ^ 1, xx, cc) if who(zz, cc) else None

    n_mine = norm_rows(latents, mod_shift, mod_scale, x)
    r1 = move(n_mine, outward(owns))
    r2a = move(n_mine, across(mid_own))

    slot_a = jnp.where(at_home, 1 - parity, parity)
    slot_b = jnp.where(at_home, parity, 1 - parity)
    msg_a = lax.dynamic_slice(w_t, (0, slot_a * heads, y * half, 0), (3, heads, half, hd))
    msg_b = lax.dynamic_slice(w_t, (0, slot_b * heads, y * half, 0), (3, heads, half, hd))
    z_a = move(msg_a, lambda yy, zz, xx, cc: (yy, zz ^ 1, xx, 1) if home(zz, cc) else (yy, zz ^ 2, xx, 0))
    z_b = move(msg_b, lambda yy, zz, xx, cc: None if home(zz, cc) else (yy, zz ^ 3, xx, zz // 2))

    tile_ids = jnp.arange(nz, dtype=jnp.int32)
    hits = jnp.any((block_list[0][:, None] == tile_ids[None]) & (block_live[0][:, None] > 0), axis=0)
    flags = jnp.concatenate([key_valid, jnp.pad(hits.astype(jnp.int32), (0, 128 - nz))])[None]
    flags = jnp.concatenate(
        [flags]
        + [move(flags, lambda yy, zz, xx, cc, d=d: (yy, zz ^ d, xx, cc)) for d in range(1, nz)]
    )

    n_other = norm_rows(latents, mod_shift, mod_scale, 1 - x)
    own_w = lax.dynamic_slice(w_t, (0, parity * heads, 0, 0), (3, heads, depth, hd))

    r2b = move(r1, across(mid_rest))
    x_r1 = move(r1, to_column(lambda zz, cc: not owns(zz, cc)))
    r3a = move(r2a, outward(mid_rest))
    x_r2a = move(r2a, to_column(mid_rest))
    r3b = move(r2b, outward(mid_own))
    x_r2b = move(r2b, to_column(mid_own))
    x_r3a = move(r3a, to_column(end_own))
    x_r3b = move(r3b, to_column(end_rest))

    y_a = move(z_a, to_replica())
    c_a1 = move(z_a, to_core())
    c_own = move(own_w, to_core(home))
    y_b = move(z_b, to_replica(lambda zz, cc: not home(zz, cc)))
    c_b1 = move(z_b, to_core(lambda zz, cc: not home(zz, cc)))
    c_a2 = move(y_a, to_core())
    c_b2 = move(y_b, to_core(lambda zz, cc: not home(zz, cc)))
    weights = (z_a, y_a, c_a1, c_a2, own_w, c_own, z_b, y_b, c_b1, c_b2)
    sources = (
        jnp.where(c == 0, z ^ 2, z ^ 1),
        jnp.where(c == 0, z ^ 1, z ^ 2),
        z,
        z ^ 3,
        y,
        x,
        at_home,
    )

    s1 = move(wo, lambda yy, zz, xx, cc: (yy, zz ^ 1, xx, zz % 2) if cc == yy else None)
    s2a = move(wo, lambda yy, zz, xx, cc: (yy, 3 - zz, xx, zz % 2) if cc == yy and mid(zz) else None)
    c_f = move(wo, to_core(lambda zz, cc: not owns(zz, cc)))
    s2b = move(s1, across(mid_rest))
    y_f = move(s1, to_replica(lambda zz, cc: not owns(zz, cc)))
    s3a = move(s2a, outward(mid_rest))
    s3b = move(s2b, outward(mid_own))
    g_z = jnp.where(is_mid, jnp.where(own, s2b, s2a), jnp.where(own, s3a, s3b))
    y_g = move(g_z, to_replica())

    q_near, kv_near = qkv_tile(
        scalars_of(*sources, jnp.where(own, 0, 1)), (n_mine, r1), (n_other, x_r1), weights, query_gain, key_gain
    )
    kv_near_o = move(kv_near, to_core())
    q_far, kv_far = qkv_tile(
        scalars_of(*sources, jnp.where(is_mid, jnp.where(own, 1, 0), jnp.where(own, 2, 3))),
        (r2a, r2b, r3a, r3b),
        (x_r2a, x_r2b, x_r3a, x_r3b),
        weights,
        query_gain,
        key_gain,
    )
    kv_far_o = move(kv_far, to_core())

    segments = (near, far, near_o, far_o)
    marks = (*segments, *(s ^ z for s in segments))
    kvs = (kv_near, kv_far, kv_near_o, kv_far_o)
    att_far = attend(scalars_of(*marks, far ^ z), q_far, kvs, flags)
    p_far = move(att_far, lambda yy, zz, xx, cc: (yy, 2 * (1 - zz // 2) + cc, xx, zz % 2))
    att_near = attend(scalars_of(*marks, near ^ z), q_near, kvs, flags)
    p_near = move(att_near, outward(lambda zz, cc: not owns(zz, cc)))
    b_near = move(att_near, to_core(owns))
    p_far_o = move(p_far, to_core())
    b_pair = move(p_near, to_core(owns))

    pieces = (att_near, b_near, p_near, b_pair, p_far, p_far_o)
    blocks = (wo, c_f, s1, y_f, g_z, y_g)
    places = (own, c, y, z, z ^ 1, far, far_o)
    send = project(scalars_of(*places, x != pair), pieces, blocks, BF16)
    got = move(send, to_column())
    keep = project(scalars_of(*places, x == pair), pieces, blocks, F32)
    projected = keep + got.astype(F32)
    out_width = projected.shape[1]
    offset = (x * nc + c) * out_width
    latent_cols = lax.dynamic_slice_in_dim(latents, offset, out_width, 1).astype(F32)
    gate_cols = lax.dynamic_slice_in_dim(mod_gate, offset, out_width, 0)
    return (latent_cols + gate_cols * projected).astype(BF16)


def modulate(latents, mod_shift, mod_scale):
    x_float = latents.astype(F32)
    centre = x_float - jnp.mean(x_float, axis=-1, keepdims=True)
    spread = jnp.mean(centre * centre, axis=-1, keepdims=True)
    return (centre * lax.rsqrt(spread + EPS) * (1.0 + mod_scale) + mod_shift).astype(BF16)


def gather_local(
    latents,
    w_qkv,
    w_out,
    query_gain,
    key_gain,
    mod_shift,
    mod_scale,
    mod_gate,
    block_list,
    block_live,
    key_valid,
):
    gather = functools.partial(lax.all_gather, axis_name="seq", tiled=True)
    tok_rows = latents.shape[0]
    tile = tok_rows // block_list.shape[0]
    tiles_all = block_list.shape[0] * lax.axis_size("seq")
    normed = modulate(latents, mod_shift, mod_scale)
    qkv = jnp.einsum("td,dshe->tshe", normed, gather(w_qkv, axis=0), preferred_element_type=F32)
    queries = head_norm(qkv[:, 0], query_gain)
    keys = gather(head_norm(qkv[:, 1], key_gain), axis=0)
    values = gather(qkv[:, 2].astype(BF16), axis=0)
    key_ok = gather(key_valid, axis=0) > 0
    tile_ids = jnp.arange(tiles_all, dtype=jnp.int32)
    hits = jnp.any(
        (block_list[:, :, None] == tile_ids[None, None, :]) & (block_live[:, :, None] > 0), axis=1
    )
    allowed = jnp.repeat(jnp.repeat(hits, tile, axis=0), tile, axis=1) & key_ok[None, :]
    scores = jnp.einsum("qhe,khe->hqk", queries, keys, preferred_element_type=F32) / math.sqrt(
        queries.shape[-1]
    )
    masked = jnp.where(allowed[None], scores, NEG)
    weights = jnp.where(allowed[None], jnp.exp(masked - jnp.max(masked, axis=2, keepdims=True)), 0.0)
    total = jnp.sum(weights, axis=2)
    weighted = jnp.einsum("hqk,khe->qhe", weights.astype(BF16), values, preferred_element_type=F32)
    attended = (weighted / jnp.transpose(total)[:, :, None]).astype(BF16)
    head_terms = jnp.einsum("the,hec->tc", attended, gather(w_out, axis=2), preferred_element_type=F32)
    projected = lax.psum_scatter(
        head_terms.astype(BF16), ("tp", "sub"), scatter_dimension=1, tiled=True
    ).astype(F32)
    out_width = projected.shape[1]
    offset = lax.axis_index(("tp", "sub")) * out_width
    latent_cols = lax.dynamic_slice_in_dim(latents, offset, out_width, 1).astype(F32)
    gate_cols = lax.dynamic_slice_in_dim(mod_gate, offset, out_width, 0)
    return (latent_cols + gate_cols * projected).astype(BF16)


def solution(mesh):
    sizes = tuple(mesh.shape[a] for a in AXES)
    ny, nz, nx, nc = sizes
    line = ny == nx == nc == 2 and nz == nc * 2

    def local(*args):
        heads_here, block_list = args[1].shape[2], args[8]
        if line and heads_here % nc == 0 and block_list.shape[0] == 1:
            return line_local(sizes, *args)
        return gather_local(*args)

    in_specs = (
        P(("rep", "seq"), None),
        P("seq", None, ("tp", "sub"), None),
        P(("tp", "sub"), None, "seq"),
        P(),
        P(),
        P("rep"),
        P("rep"),
        P("rep"),
        P(("rep", "seq"), None),
        P(("rep", "seq"), None),
        P(("rep", "seq")),
    )
    out_specs = P(("rep", "seq"), ("tp", "sub"))
    return jax.shard_map(local, mesh=mesh, in_specs=in_specs, out_specs=out_specs, check_vma=False)
```

```python
import functools
import math

import jax
import jax.numpy as jnp
from jax import lax
from jax.experimental import pallas as pl
from jax.experimental.pallas import tpu as pltpu
from jax.sharding import PartitionSpec as P


AXES = ("rep", "seq", "tp", "sub")
EPS = 1e-06
NEG = -1e30
F32 = jnp.float32
BF16 = jnp.bfloat16


def norm_kernel(half_ref, x_ref, shift_ref, scale_ref, out_ref):
    x_float = x_ref[...].astype(F32)
    centre = x_float - jnp.mean(x_float, axis=-1, keepdims=True)
    spread = jnp.mean(centre * centre, axis=-1, keepdims=True)
    scaled = centre * lax.rsqrt(spread + EPS) * (1.0 + scale_ref[...])
    out_ref[...] = (scaled + shift_ref[...]).astype(BF16)


def norm_rows(latents, mod_shift, mod_scale, half):
    rows, width = latents.shape
    steps = 4
    block = rows // 2 // steps
    vector = pl.BlockSpec((1, width), lambda i, half_ref: (0, 0))
    return pl.pallas_call(
        norm_kernel,
        out_shape=jax.ShapeDtypeStruct((rows // 2, width), BF16),
        grid_spec=pltpu.PrefetchScalarGridSpec(
            num_scalar_prefetch=1,
            grid=(steps,),
            in_specs=[
                pl.BlockSpec((block, width), lambda i, half_ref: (half_ref[0] * steps + i, 0)),
                vector,
                vector,
            ],
            out_specs=pl.BlockSpec((block, width), lambda i, half_ref: (i, 0)),
        ),
        cost_estimate=pl.CostEstimate(flops=rows * width * 5, bytes_accessed=rows * width * 2, transcendentals=rows),
        name="norm_rows",
    )(half[None], latents, mod_shift[None], mod_scale[None])


def head_norm(raw, gain):
    square = jnp.mean(raw * raw, axis=-1, keepdims=True)
    return (raw * lax.rsqrt(square + EPS) * gain).astype(BF16)


def qkv_kernel(counts, sc_ref, *refs):
    tiles = []
    for count in counts:
        tiles.append((refs[:count], refs[count : 2 * count]))
        refs = refs[2 * count :]
    za, ya, ca1, ca2, own_w, own_c, zb, yb, cb1, cb2, gq_ref, gk_ref = refs[:12]
    q_ref, kv_ref, tok_ref, w_ref, acc_ref, gain_ref, tok_sem, w_sem, gain_sem = refs[12:]
    half_rows = tiles[0][0][0].shape[0]
    _, heads, depth, hd = za.shape
    col, rep, at_home = sc_ref[5], sc_ref[4], sc_ref[6] == 1
    bases = [pl.multiple_of(sc_ref[i] * (2 * depth), 128) for i in range(4)]

    def tok_copy(ref, block, tile, i):
        start = pl.multiple_of((col if i == 0 else 1 - col) * half_rows, 64)
        cols = pl.ds(bases[block], 2 * depth)
        dst = tok_ref.at[tile, pl.ds(start, half_rows), cols]
        return pltpu.make_async_copy(ref.at[:, cols], dst, tok_sem.at[block, tile, i])

    def w_copy(ref, block, i):
        if i is None:
            start, size, sem = bases[block], 2 * depth, w_sem.at[2 * block]
        else:
            start, size, sem = bases[block] + (rep if i == 0 else 1 - rep) * depth, depth, w_sem.at[2 * block + i]
        return pltpu.make_async_copy(ref, w_ref.at[:, :, pl.ds(pl.multiple_of(start, 128), size), :], sem)

    def when_home(home, away):
        @pl.when(at_home)
        def _():
            for copy in home:
                copy.start()

        @pl.when(jnp.logical_not(at_home))
        def _():
            for copy in away:
                copy.start()

        return home

    def fetch_weights(block):
        if block == 2:
            return when_home([w_copy(own_w, 2, None)], [w_copy(own_c, 2, None)])
        if block == 3:
            return when_home([w_copy(cb1, 3, 0), w_copy(cb2, 3, 1)], [w_copy(zb, 3, 0), w_copy(yb, 3, 1)])
        pair = (za, ya) if block == 0 else (ca1, ca2)
        copies = [w_copy(pair[0], block, 0), w_copy(pair[1], block, 1)]
        for copy in copies:
            copy.start()
        return copies

    def fetch(block):
        for tile, (mine, others) in enumerate(tiles):
            for i in range(counts[tile]):

                @pl.when(sc_ref[7 + tile] == i)
                def _():
                    tok_copy(mine[i], block, tile, 0).start()
                    tok_copy(others[i], block, tile, 1).start()

        waits = fetch_weights(block)
        return waits + [tok_copy(pairs[0], block, tile, i) for tile, t in enumerate(tiles) for i, pairs in enumerate(t)]

    gains = [pltpu.make_async_copy(r, gain_ref.at[i], gain_sem.at[i]) for i, r in enumerate((gq_ref, gk_ref))]
    waits = {0: fetch(0), 1: fetch(1)}
    for copy in gains:
        copy.start()
    for block in range(4):
        for copy in waits[block]:
            copy.wait()
        if block + 2 < 4:
            waits[block + 2] = fetch(block + 2)
        part = pl.ds(bases[block], 2 * depth)
        w = jnp.concatenate([w_ref[s, h, part, :] for s in range(3) for h in range(heads)], axis=1)
        for tile in range(2):
            term = jnp.dot(tok_ref[tile, :, part], w, preferred_element_type=F32)
            acc_ref[tile] = term if block == 0 else acc_ref[tile] + term

    for copy in gains:
        copy.wait()
    for tile in range(2):
        for h in range(heads):
            lanes = slice(h * hd, (h + 1) * hd)
            q_ref[tile, :, lanes] = head_norm(acc_ref[tile, :, lanes], gain_ref[0])
            kv_ref[tile, :, lanes] = head_norm(acc_ref[tile, :, (heads + h) * hd : (heads + h + 1) * hd], gain_ref[1])
        kv_ref[tile, :, heads * hd :] = acc_ref[tile, :, 2 * heads * hd :].astype(BF16)


def qkv_tiles(scalars, candidates, weights, query_gain, key_gain):
    half_rows, width = candidates[0][0][0].shape
    _, heads, _, hd = weights[0].shape
    rows, out = 2 * half_rows, heads * hd
    counts = tuple(len(mine) for mine, _ in candidates)
    tokens = [t for mine, others in candidates for t in (*mine, *others)]
    smem = pl.BlockSpec(memory_space=pltpu.SMEM)
    vmem = pl.BlockSpec(memory_space=pltpu.VMEM)
    anywhere = pl.BlockSpec(memory_space=pl.ANY)
    return pl.pallas_call(
        functools.partial(qkv_kernel, counts),
        out_shape=(
            jax.ShapeDtypeStruct((2, rows, out), BF16),
            jax.ShapeDtypeStruct((2, rows, 2 * out), BF16),
        ),
        in_specs=[smem] + [anywhere] * (len(tokens) + len(weights) + 2),
        out_specs=(vmem, vmem),
        scratch_shapes=[
            pltpu.VMEM((2, rows, width), BF16),
            pltpu.VMEM((3, heads, width, hd), BF16),
            pltpu.VMEM((2, rows, 3 * out), F32),
            pltpu.VMEM((2, 1, hd), F32),
            pltpu.SemaphoreType.DMA((4, 2, 2)),
            pltpu.SemaphoreType.DMA((8,)),
            pltpu.SemaphoreType.DMA((2,)),
        ],
        cost_estimate=pl.CostEstimate(
            flops=12 * rows * width * out, bytes_accessed=width * 3 * out * 2, transcendentals=0
        ),
        name="qkv_tiles",
    )(scalars, *tokens, *weights, query_gain[None], key_gain[None])


def attend_kernel(sc_ref, q_ref, kv0, kv1, flags_ref, near_ref, far_ref):
    _, rows, width = q_ref.shape
    hd = 128
    heads = width // hd
    factor = math.log2(math.e) / math.sqrt(hd)
    flags = flags_ref[...]
    place = lax.broadcasted_iota(jnp.int32, flags.shape, 0)
    segments = ((kv0, 0), (kv0, 1), (kv1, 0), (kv1, 1))

    def row(d):
        return jnp.sum(jnp.where(place == d, flags, 0), axis=0, keepdims=True)

    rows_of = [row(sc_ref[4 + s]) for s in range(4)]
    biases = []
    for t in range(2):
        hits = rows_of[t][:, rows:]
        lane = lax.broadcasted_iota(jnp.int32, hits.shape, 1)
        bias = []
        for s in range(4):
            hit = jnp.sum(jnp.where(lane == sc_ref[s], hits, 0), axis=1, keepdims=True)
            bias.append(jnp.where(rows_of[s][:, :rows] * hit > 0, 0.0, NEG).astype(F32))
        biases.append(jnp.concatenate(bias, axis=1))
    for t, out_ref in ((1, far_ref), (0, near_ref)):
        for h in range(heads):
            lanes = slice(h * hd, (h + 1) * hd)
            keys = jnp.concatenate([r[s, :, lanes] for r, s in segments], axis=0)
            vals = jnp.concatenate([r[s, :, width + h * hd : width + (h + 1) * hd] for r, s in segments], axis=0)
            scores = lax.dot_general(
                q_ref[t, :, lanes], keys, (((1,), (1,)), ((), ())), preferred_element_type=F32
            )
            scores = scores * factor + biases[t]
            weights = jnp.exp2(scores - jnp.max(scores, axis=1, keepdims=True))
            total = jnp.sum(weights, axis=1, keepdims=True)
            added = jnp.dot(weights.astype(BF16), vals, preferred_element_type=F32)
            out_ref[:, lanes] = (added / total).astype(BF16)


def attend(scalars, queries, kv, kv_other, flags):
    _, rows, width = queries.shape
    smem = pl.BlockSpec(memory_space=pltpu.SMEM)
    vmem = pl.BlockSpec(memory_space=pltpu.VMEM)
    keys = 4 * rows
    shape = jax.ShapeDtypeStruct((rows, width), BF16)
    return pl.pallas_call(
        attend_kernel,
        out_shape=(shape, shape),
        in_specs=[smem] + [vmem] * 4,
        out_specs=(vmem, vmem),
        compiler_params=pltpu.CompilerParams(vmem_limit_bytes=24 << 20),
        cost_estimate=pl.CostEstimate(
            flops=8 * rows * keys * width, bytes_accessed=8 * rows * width * 2, transcendentals=2 * rows * keys * width // 128
        ),
        name="attend",
    )(scalars, queries, kv, kv_other, flags)


def project_kernel(sc_ref, an, bn, ap, bp, f0, f1, *refs):
    firsts, seconds = refs[0:12:2], refs[1:12:2]
    out_ref, att_ref, w_ref, att_sem, w_sem = refs[12:]
    _, width = an.shape
    depth = w_ref.shape[1]

    def piece_copy(ref, i):
        lanes = pl.ds(pl.multiple_of(sc_ref[1 + i] * width, 128), width)
        return pltpu.make_async_copy(ref, att_ref.at[:, lanes], att_sem.at[i])

    @pl.when(sc_ref[0] == 1)
    def _():
        piece_copy(an, 0).start()
        piece_copy(ap, 1).start()

    @pl.when(sc_ref[0] == 0)
    def _():
        piece_copy(bn, 0).start()
        piece_copy(bp, 1).start()

    piece_copy(f0, 2).start()
    piece_copy(f1, 3).start()
    for i in range(6):

        @pl.when(sc_ref[5] == i)
        def _():
            pltpu.make_async_copy(firsts[i], w_ref.at[0], w_sem.at[0]).start()
            pltpu.make_async_copy(seconds[i], w_ref.at[1], w_sem.at[1]).start()

    for i in range(4):
        piece_copy(f0, i).wait()
    terms = []
    for i in range(2):
        group = sc_ref[6] if i == 0 else 1 - sc_ref[6]
        pltpu.make_async_copy(firsts[0], w_ref.at[i], w_sem.at[i]).wait()
        part = att_ref[:, pl.ds(pl.multiple_of(group * depth, 128), depth)]
        terms.append(jnp.dot(part, w_ref[i], preferred_element_type=F32).astype(BF16).astype(F32))
    out_ref[...] = (terms[0] + terms[1]).astype(out_ref.dtype)


def project(scalars, pieces, weights, dtype):
    rows = pieces[0].shape[0]
    depth, width = weights[0].shape
    smem = pl.BlockSpec(memory_space=pltpu.SMEM)
    vmem = pl.BlockSpec(memory_space=pltpu.VMEM)
    anywhere = pl.BlockSpec(memory_space=pl.ANY)
    return pl.pallas_call(
        project_kernel,
        out_shape=jax.ShapeDtypeStruct((rows, width), dtype),
        in_specs=[smem] + [anywhere] * (len(pieces) + len(weights)),
        out_specs=vmem,
        scratch_shapes=[
            pltpu.VMEM((rows, 2 * depth), BF16),
            pltpu.VMEM((2, depth, width), BF16),
            pltpu.SemaphoreType.DMA((4,)),
            pltpu.SemaphoreType.DMA((2,)),
        ],
        compiler_params=pltpu.CompilerParams(vmem_limit_bytes=16 << 20),
        cost_estimate=pl.CostEstimate(
            flops=4 * rows * depth * width, bytes_accessed=4 * depth * width * 2, transcendentals=0
        ),
        name="project",
    )(scalars, *pieces, *weights)


def scalars_of(*values):
    return jnp.stack([jnp.asarray(v, jnp.int32) for v in values])


def line_local(
    sizes,
    latents,
    w_qkv,
    w_out,
    query_gain,
    key_gain,
    mod_shift,
    mod_scale,
    mod_gate,
    block_list,
    block_live,
    key_valid,
):
    ny, nz, nx, nc = sizes
    y, z, x, c = (lax.axis_index(a) for a in AXES)

    def move(array, target):
        pairs = []
        for yy in range(ny):
            for zz in range(nz):
                for xx in range(nx):
                    for cc in range(nc):
                        to = target(yy, zz, xx, cc)
                        if to is not None:
                            flat = lambda p: ((p[0] * nz + p[1]) * nx + p[2]) * nc + p[3]
                            pairs.append((flat((yy, zz, xx, cc)), flat(to)))
        return lax.ppermute(array, AXES, pairs)

    def owns(zz, cc):
        return zz % 2 == cc

    def home(zz, cc):
        return zz // 2 == cc

    def mid(zz):
        return zz in (1, 2)

    def to_core(who=lambda zz, cc: True):
        return lambda yy, zz, xx, cc: (yy, zz, xx, 1 - cc) if who(zz, cc) else None

    def to_column(who=lambda zz, cc: True):
        return lambda yy, zz, xx, cc: (yy, zz, 1 - xx, cc) if who(zz, cc) else None

    def to_replica(who=lambda zz, cc: True):
        return lambda yy, zz, xx, cc: (1 - yy, zz, xx, cc) if who(zz, cc) else None

    own = z % 2 == c
    at_home = z // 2 == c
    is_mid = (z == 1) | (z == 2)
    pair = z // 2
    parity = z % 2
    near, far = 2 * pair + c, 2 * (1 - pair) + c
    near_o, far_o = 2 * pair + 1 - c, 2 * (1 - pair) + 1 - c

    depth, _, heads_here, hd = w_qkv.shape
    heads = heads_here * nc // nz
    half = depth // 2
    w_t = jnp.transpose(w_qkv, (1, 2, 0, 3))
    wo = w_out.reshape(heads_here * hd, w_out.shape[2])

    def mid_own(zz, cc):
        return mid(zz) and owns(zz, cc)

    def mid_rest(zz, cc):
        return mid(zz) and not owns(zz, cc)

    def end_own(zz, cc):
        return not mid(zz) and owns(zz, cc)

    def end_rest(zz, cc):
        return not mid(zz) and not owns(zz, cc)

    def across(who):
        return lambda yy, zz, xx, cc: (yy, 3 - zz, xx, cc) if who(zz, cc) else None

    def outward(who):
        return lambda yy, zz, xx, cc: (yy, zz ^ 1, xx, cc) if who(zz, cc) else None

    n_mine = norm_rows(latents, mod_shift, mod_scale, x)
    r1 = move(n_mine, outward(owns))
    r2a = move(n_mine, across(mid_own))

    slot_a = jnp.where(at_home, 1 - parity, parity)
    slot_b = jnp.where(at_home, parity, 1 - parity)
    msg_a = lax.dynamic_slice(w_t, (0, slot_a * heads, y * half, 0), (3, heads, half, hd))
    msg_b = lax.dynamic_slice(w_t, (0, slot_b * heads, y * half, 0), (3, heads, half, hd))
    z_a = move(msg_a, lambda yy, zz, xx, cc: (yy, zz ^ 1, xx, 1) if home(zz, cc) else (yy, zz ^ 2, xx, 0))
    z_b = move(msg_b, lambda yy, zz, xx, cc: None if home(zz, cc) else (yy, zz ^ 3, xx, zz // 2))

    tile_ids = jnp.arange(nz, dtype=jnp.int32)
    hits = jnp.any((block_list[0][:, None] == tile_ids[None]) & (block_live[0][:, None] > 0), axis=0)
    flags = jnp.concatenate([key_valid, jnp.pad(hits.astype(jnp.int32), (0, 128 - nz))])[None]
    flags = jnp.concatenate(
        [flags]
        + [move(flags, lambda yy, zz, xx, cc, d=d: (yy, zz ^ d, xx, cc)) for d in range(1, nz)]
    )

    n_other = norm_rows(latents, mod_shift, mod_scale, 1 - x)
    own_w = lax.dynamic_slice(w_t, (0, parity * heads, 0, 0), (3, heads, depth, hd))

    r2b = move(r1, across(mid_rest))
    x_r1 = move(r1, to_column(lambda zz, cc: not owns(zz, cc)))
    r3a = move(r2a, outward(mid_rest))
    x_r2a = move(r2a, to_column(mid_rest))
    r3b = move(r2b, outward(mid_own))
    x_r2b = move(r2b, to_column(mid_own))
    x_r3a = move(r3a, to_column(end_own))
    x_r3b = move(r3b, to_column(end_rest))

    y_a = move(z_a, to_replica())
    c_a1 = move(z_a, to_core())
    c_own = move(own_w, to_core(home))
    y_b = move(z_b, to_replica(lambda zz, cc: not home(zz, cc)))
    c_b1 = move(z_b, to_core(lambda zz, cc: not home(zz, cc)))
    c_a2 = move(y_a, to_core())
    c_b2 = move(y_b, to_core(lambda zz, cc: not home(zz, cc)))
    weights = (z_a, y_a, c_a1, c_a2, own_w, c_own, z_b, y_b, c_b1, c_b2)
    sources = (
        jnp.where(c == 0, z ^ 2, z ^ 1),
        jnp.where(c == 0, z ^ 1, z ^ 2),
        z,
        z ^ 3,
        y,
        x,
        at_home,
    )

    s1 = move(wo, lambda yy, zz, xx, cc: (yy, zz ^ 1, xx, zz % 2) if cc == yy else None)
    s2a = move(wo, lambda yy, zz, xx, cc: (yy, 3 - zz, xx, zz % 2) if cc == yy and mid(zz) else None)
    c_f = move(wo, to_core(lambda zz, cc: not owns(zz, cc)))
    s2b = move(s1, across(mid_rest))
    y_f = move(s1, to_replica(lambda zz, cc: not owns(zz, cc)))
    s3a = move(s2a, outward(mid_rest))
    s3b = move(s2b, outward(mid_own))
    y_2a = move(s2a, to_replica(mid_rest))
    y_2b = move(s2b, to_replica(mid_own))
    y_3a = move(s3a, to_replica(end_own))
    y_3b = move(s3b, to_replica(end_rest))

    picks = (jnp.where(own, 0, 1), jnp.where(is_mid, jnp.where(own, 1, 0), jnp.where(own, 2, 3)))
    queries, kv = qkv_tiles(
        scalars_of(*sources, *picks),
        (((n_mine, r1), (n_other, x_r1)), ((r2a, r2b, r3a, r3b), (x_r2a, x_r2b, x_r3a, x_r3b))),
        weights,
        query_gain,
        key_gain,
    )
    kv_other = move(kv, to_core())

    segments = (near, far, near_o, far_o)
    att_near, att_far = attend(scalars_of(*segments, *(s ^ z for s in segments)), queries, kv, kv_other, flags)
    p_far = move(att_far, lambda yy, zz, xx, cc: (yy, 2 * (1 - zz // 2) + cc, xx, zz % 2))
    p_near = move(att_near, outward(lambda zz, cc: not owns(zz, cc)))
    b_near = move(att_near, to_core(owns))
    p_far_o = move(p_far, to_core())
    b_pair = move(p_near, to_core(owns))

    pieces = (att_near, b_near, p_near, b_pair, p_far, p_far_o)
    blocks = (wo, c_f, s1, y_f, s2a, y_2a, s2b, y_2b, s3a, y_3a, s3b, y_3b)
    places = (own, z, z ^ 1, far, far_o)
    from_near = (jnp.where(own, 0, 1), jnp.where(own, c, y))
    from_far = (2 + jnp.where(is_mid, jnp.where(own, 1, 0), jnp.where(own, 2, 3)), y)
    near_stays = x == pair

    def project_block(near_block):
        chosen = [jnp.where(near_block, n, f) for n, f in zip(from_near, from_far)]
        return scalars_of(*places, *chosen)

    send = project(project_block(jnp.logical_not(near_stays)), pieces, blocks, BF16)
    got = move(send, to_column())
    keep = project(project_block(near_stays), pieces, blocks, F32)
    projected = keep + got.astype(F32)
    out_width = projected.shape[1]
    offset = (x * nc + c) * out_width
    latent_cols = lax.dynamic_slice_in_dim(latents, offset, out_width, 1).astype(F32)
    gate_cols = lax.dynamic_slice_in_dim(mod_gate, offset, out_width, 0)
    return (latent_cols + gate_cols * projected).astype(BF16)


def modulate(latents, mod_shift, mod_scale):
    x_float = latents.astype(F32)
    centre = x_float - jnp.mean(x_float, axis=-1, keepdims=True)
    spread = jnp.mean(centre * centre, axis=-1, keepdims=True)
    return (centre * lax.rsqrt(spread + EPS) * (1.0 + mod_scale) + mod_shift).astype(BF16)


def gather_local(
    latents,
    w_qkv,
    w_out,
    query_gain,
    key_gain,
    mod_shift,
    mod_scale,
    mod_gate,
    block_list,
    block_live,
    key_valid,
):
    gather = functools.partial(lax.all_gather, axis_name="seq", tiled=True)
    tok_rows = latents.shape[0]
    tile = tok_rows // block_list.shape[0]
    tiles_all = block_list.shape[0] * lax.axis_size("seq")
    normed = modulate(latents, mod_shift, mod_scale)
    qkv = jnp.einsum("td,dshe->tshe", normed, gather(w_qkv, axis=0), preferred_element_type=F32)
    queries = head_norm(qkv[:, 0], query_gain)
    keys = gather(head_norm(qkv[:, 1], key_gain), axis=0)
    values = gather(qkv[:, 2].astype(BF16), axis=0)
    key_ok = gather(key_valid, axis=0) > 0
    tile_ids = jnp.arange(tiles_all, dtype=jnp.int32)
    hits = jnp.any(
        (block_list[:, :, None] == tile_ids[None, None, :]) & (block_live[:, :, None] > 0), axis=1
    )
    allowed = jnp.repeat(jnp.repeat(hits, tile, axis=0), tile, axis=1) & key_ok[None, :]
    scores = jnp.einsum("qhe,khe->hqk", queries, keys, preferred_element_type=F32) / math.sqrt(
        queries.shape[-1]
    )
    masked = jnp.where(allowed[None], scores, NEG)
    weights = jnp.where(allowed[None], jnp.exp(masked - jnp.max(masked, axis=2, keepdims=True)), 0.0)
    total = jnp.sum(weights, axis=2)
    weighted = jnp.einsum("hqk,khe->qhe", weights.astype(BF16), values, preferred_element_type=F32)
    attended = (weighted / jnp.transpose(total)[:, :, None]).astype(BF16)
    head_terms = jnp.einsum("the,hec->tc", attended, gather(w_out, axis=2), preferred_element_type=F32)
    projected = lax.psum_scatter(
        head_terms.astype(BF16), ("tp", "sub"), scatter_dimension=1, tiled=True
    ).astype(F32)
    out_width = projected.shape[1]
    offset = lax.axis_index(("tp", "sub")) * out_width
    latent_cols = lax.dynamic_slice_in_dim(latents, offset, out_width, 1).astype(F32)
    gate_cols = lax.dynamic_slice_in_dim(mod_gate, offset, out_width, 0)
    return (latent_cols + gate_cols * projected).astype(BF16)


def solution(mesh):
    sizes = tuple(mesh.shape[a] for a in AXES)
    ny, nz, nx, nc = sizes
    line = ny == nx == nc == 2 and nz == nc * 2

    def local(*args):
        heads_here, block_list = args[1].shape[2], args[8]
        if line and heads_here % nc == 0 and block_list.shape[0] == 1:
            return line_local(sizes, *args)
        return gather_local(*args)

    in_specs = (
        P(("rep", "seq"), None),
        P("seq", None, ("tp", "sub"), None),
        P(("tp", "sub"), None, "seq"),
        P(),
        P(),
        P("rep"),
        P("rep"),
        P("rep"),
        P(("rep", "seq"), None),
        P(("rep", "seq"), None),
        P(("rep", "seq")),
    )
    out_specs = P(("rep", "seq"), ("tp", "sub"))
    return jax.shard_map(local, mesh=mesh, in_specs=in_specs, out_specs=out_specs, check_vma=False)
```

```python
import functools
import math

import jax
import jax.numpy as jnp
from jax import lax
from jax.experimental import pallas as pl
from jax.experimental.pallas import tpu as pltpu
from jax.sharding import PartitionSpec as P


AXES = ("rep", "seq", "tp", "sub")
EPS = 1e-06
NEG = -1e30
F32 = jnp.float32
BF16 = jnp.bfloat16


def norm_kernel(half_ref, x_ref, shift_ref, scale_ref, out_ref):
    x_float = x_ref[...].astype(F32)
    centre = x_float - jnp.mean(x_float, axis=-1, keepdims=True)
    spread = jnp.mean(centre * centre, axis=-1, keepdims=True)
    scaled = centre * lax.rsqrt(spread + EPS) * (1.0 + scale_ref[...])
    out_ref[...] = (scaled + shift_ref[...]).astype(BF16)


def norm_rows(latents, mod_shift, mod_scale, half):
    rows, width = latents.shape
    steps = 4
    block = rows // 2 // steps
    vector = pl.BlockSpec((1, width), lambda i, half_ref: (0, 0))
    return pl.pallas_call(
        norm_kernel,
        out_shape=jax.ShapeDtypeStruct((rows // 2, width), BF16),
        grid_spec=pltpu.PrefetchScalarGridSpec(
            num_scalar_prefetch=1,
            grid=(steps,),
            in_specs=[
                pl.BlockSpec((block, width), lambda i, half_ref: (half_ref[0] * steps + i, 0)),
                vector,
                vector,
            ],
            out_specs=pl.BlockSpec((block, width), lambda i, half_ref: (i, 0)),
        ),
        cost_estimate=pl.CostEstimate(flops=rows * width * 5, bytes_accessed=rows * width * 2, transcendentals=rows),
        name="norm_rows",
    )(half[None], latents, mod_shift[None], mod_scale[None])


def head_norm(raw, gain):
    square = jnp.mean(raw * raw, axis=-1, keepdims=True)
    return (raw * lax.rsqrt(square + EPS) * gain).astype(BF16)


def qkv_kernel(counts, sc_ref, *refs):
    tiles = []
    for count in counts:
        tiles.append((refs[:count], refs[count : 2 * count]))
        refs = refs[2 * count :]
    za, ya, ca1, ca2, own_w, own_c, zb, yb, cb1, cb2, gq_ref, gk_ref = refs[:12]
    q_ref, kv_ref, tok_ref, w_ref, acc_ref, gain_ref, tok_sem, w_sem, gain_sem = refs[12:]
    half_rows = tiles[0][0][0].shape[0]
    _, heads, depth, hd = za.shape
    col, rep, at_home = sc_ref[5], sc_ref[4], sc_ref[6] == 1
    bases = [pl.multiple_of(sc_ref[i] * (2 * depth), 128) for i in range(4)]

    def tok_copy(ref, block, tile, i):
        start = pl.multiple_of((col if i == 0 else 1 - col) * half_rows, 64)
        cols = pl.ds(bases[block], 2 * depth)
        dst = tok_ref.at[tile, pl.ds(start, half_rows), cols]
        return pltpu.make_async_copy(ref.at[:, cols], dst, tok_sem.at[block, tile, i])

    def w_copy(ref, block, i):
        if i is None:
            start, size, sem = bases[block], 2 * depth, w_sem.at[2 * block]
        else:
            start, size, sem = bases[block] + (rep if i == 0 else 1 - rep) * depth, depth, w_sem.at[2 * block + i]
        return pltpu.make_async_copy(ref, w_ref.at[:, :, pl.ds(pl.multiple_of(start, 128), size), :], sem)

    def when_home(home, away):
        @pl.when(at_home)
        def _():
            for copy in home:
                copy.start()

        @pl.when(jnp.logical_not(at_home))
        def _():
            for copy in away:
                copy.start()

        return home

    def fetch_weights(block):
        if block == 2:
            return when_home([w_copy(own_w, 2, None)], [w_copy(own_c, 2, None)])
        if block == 3:
            return when_home([w_copy(cb1, 3, 0), w_copy(cb2, 3, 1)], [w_copy(zb, 3, 0), w_copy(yb, 3, 1)])
        pair = (za, ya) if block == 0 else (ca1, ca2)
        copies = [w_copy(pair[0], block, 0), w_copy(pair[1], block, 1)]
        for copy in copies:
            copy.start()
        return copies

    def fetch(block):
        for tile, (mine, others) in enumerate(tiles):
            for i in range(counts[tile]):

                @pl.when(sc_ref[7 + tile] == i)
                def _():
                    tok_copy(mine[i], block, tile, 0).start()
                    tok_copy(others[i], block, tile, 1).start()

        waits = fetch_weights(block)
        return waits + [tok_copy(pairs[0], block, tile, i) for tile, t in enumerate(tiles) for i, pairs in enumerate(t)]

    gains = [pltpu.make_async_copy(r, gain_ref.at[i], gain_sem.at[i]) for i, r in enumerate((gq_ref, gk_ref))]
    waits = {0: fetch(0), 1: fetch(1)}
    for copy in gains:
        copy.start()
    for block in range(4):
        for copy in waits[block]:
            copy.wait()
        if block + 2 < 4:
            waits[block + 2] = fetch(block + 2)
        part = pl.ds(bases[block], 2 * depth)
        w = jnp.concatenate([w_ref[s, h, part, :] for s in range(3) for h in range(heads)], axis=1)
        for tile in range(2):
            term = jnp.dot(tok_ref[tile, :, part], w, preferred_element_type=F32)
            acc_ref[tile] = term if block == 0 else acc_ref[tile] + term

    for copy in gains:
        copy.wait()
    for tile in range(2):
        for h in range(heads):
            lanes = slice(h * hd, (h + 1) * hd)
            q_ref[tile, :, lanes] = head_norm(acc_ref[tile, :, lanes], gain_ref[0])
            kv_ref[tile, :, lanes] = head_norm(acc_ref[tile, :, (heads + h) * hd : (heads + h + 1) * hd], gain_ref[1])
        kv_ref[tile, :, heads * hd :] = acc_ref[tile, :, 2 * heads * hd :].astype(BF16)


def qkv_tiles(scalars, candidates, weights, query_gain, key_gain):
    half_rows, width = candidates[0][0][0].shape
    _, heads, _, hd = weights[0].shape
    rows, out = 2 * half_rows, heads * hd
    counts = tuple(len(mine) for mine, _ in candidates)
    tokens = [t for mine, others in candidates for t in (*mine, *others)]
    smem = pl.BlockSpec(memory_space=pltpu.SMEM)
    vmem = pl.BlockSpec(memory_space=pltpu.VMEM)
    anywhere = pl.BlockSpec(memory_space=pltpu.HBM)
    return pl.pallas_call(
        functools.partial(qkv_kernel, counts),
        out_shape=(
            jax.ShapeDtypeStruct((2, rows, out), BF16),
            jax.ShapeDtypeStruct((2, rows, 2 * out), BF16),
        ),
        in_specs=[smem] + [anywhere] * (len(tokens) + len(weights) + 2),
        out_specs=(vmem, vmem),
        scratch_shapes=[
            pltpu.VMEM((2, rows, width), BF16),
            pltpu.VMEM((3, heads, width, hd), BF16),
            pltpu.VMEM((2, rows, 3 * out), F32),
            pltpu.VMEM((2, 1, hd), F32),
            pltpu.SemaphoreType.DMA((4, 2, 2)),
            pltpu.SemaphoreType.DMA((8,)),
            pltpu.SemaphoreType.DMA((2,)),
        ],
        compiler_params=pltpu.CompilerParams(vmem_limit_bytes=28 << 20),
        cost_estimate=pl.CostEstimate(
            flops=12 * rows * width * out, bytes_accessed=width * 3 * out * 2, transcendentals=0
        ),
        name="qkv_tiles",
    )(scalars, *tokens, *weights, query_gain[None], key_gain[None])


def attend_kernel(sc_ref, q_ref, kv0, kv1, flags_ref, near_ref, far_ref):
    _, rows, width = q_ref.shape
    hd = 128
    heads = width // hd
    factor = math.log2(math.e) / math.sqrt(hd)
    flags = flags_ref[...]
    place = lax.broadcasted_iota(jnp.int32, flags.shape, 0)
    segments = ((kv0, 0), (kv0, 1), (kv1, 0), (kv1, 1))

    def row(d):
        return jnp.sum(jnp.where(place == d, flags, 0), axis=0, keepdims=True)

    rows_of = [row(sc_ref[4 + s]) for s in range(4)]
    biases = []
    for t in range(2):
        hits = rows_of[t][:, rows:]
        lane = lax.broadcasted_iota(jnp.int32, hits.shape, 1)
        bias = []
        for s in range(4):
            hit = jnp.sum(jnp.where(lane == sc_ref[s], hits, 0), axis=1, keepdims=True)
            bias.append(jnp.where(rows_of[s][:, :rows] * hit > 0, 0.0, NEG).astype(F32))
        biases.append(jnp.concatenate(bias, axis=1))
    for t, out_ref in ((1, far_ref), (0, near_ref)):
        for h in range(heads):
            lanes = slice(h * hd, (h + 1) * hd)
            keys = jnp.concatenate([r[s, :, lanes] for r, s in segments], axis=0)
            vals = jnp.concatenate([r[s, :, width + h * hd : width + (h + 1) * hd] for r, s in segments], axis=0)
            scores = lax.dot_general(
                q_ref[t, :, lanes], keys, (((1,), (1,)), ((), ())), preferred_element_type=F32
            )
            scores = scores * factor + biases[t]
            weights = jnp.exp2(scores - jnp.max(scores, axis=1, keepdims=True))
            total = jnp.sum(weights, axis=1, keepdims=True)
            added = jnp.dot(weights.astype(BF16), vals, preferred_element_type=F32)
            out_ref[:, lanes] = (added / total).astype(BF16)


def attend(scalars, queries, kv, kv_other, flags):
    _, rows, width = queries.shape
    smem = pl.BlockSpec(memory_space=pltpu.SMEM)
    vmem = pl.BlockSpec(memory_space=pltpu.VMEM)
    keys = 4 * rows
    shape = jax.ShapeDtypeStruct((rows, width), BF16)
    return pl.pallas_call(
        attend_kernel,
        out_shape=(shape, shape),
        in_specs=[smem] + [vmem] * 4,
        out_specs=(vmem, vmem),
        compiler_params=pltpu.CompilerParams(vmem_limit_bytes=24 << 20),
        cost_estimate=pl.CostEstimate(
            flops=8 * rows * keys * width, bytes_accessed=8 * rows * width * 2, transcendentals=2 * rows * keys * width // 128
        ),
        name="attend",
    )(scalars, queries, kv, kv_other, flags)


def project_kernel(sc_ref, an, pn, bp, f0, f1, *refs):
    firsts, seconds = refs[0:10:2], refs[1:10:2]
    out_ref, att_ref, w_ref, att_sem, w_sem = refs[10:]
    _, width = an.shape
    depth = w_ref.shape[1]

    def piece_copy(ref, i):
        lanes = pl.ds(pl.multiple_of(sc_ref[1 + i] * width, 128), width)
        return pltpu.make_async_copy(ref, att_ref.at[:, lanes], att_sem.at[i])

    @pl.when(sc_ref[0] == 1)
    def _():
        piece_copy(an, 0).start()
        piece_copy(pn, 1).start()

    @pl.when(sc_ref[0] == 0)
    def _():
        piece_copy(pn, 0).start()
        piece_copy(bp, 1).start()

    piece_copy(f0, 2).start()
    piece_copy(f1, 3).start()
    for i in range(5):

        @pl.when(sc_ref[5] == i)
        def _():
            pltpu.make_async_copy(firsts[i], w_ref.at[0], w_sem.at[0]).start()

    for i in range(4):
        piece_copy(f0, i).wait()
    for i in range(5):

        @pl.when(sc_ref[5] == i)
        def _():
            pltpu.make_async_copy(seconds[i], w_ref.at[1], w_sem.at[1]).start()

    terms = []
    for i in range(2):
        group = sc_ref[6] if i == 0 else 1 - sc_ref[6]
        pltpu.make_async_copy(firsts[0], w_ref.at[i], w_sem.at[i]).wait()
        part = att_ref[:, pl.ds(pl.multiple_of(group * depth, 128), depth)]
        terms.append(jnp.dot(part, w_ref[i], preferred_element_type=F32).astype(BF16).astype(F32))
    out_ref[...] = (terms[0] + terms[1]).astype(out_ref.dtype)


def project(scalars, pieces, weights, dtype):
    rows = pieces[0].shape[0]
    depth, width = weights[0].shape
    smem = pl.BlockSpec(memory_space=pltpu.SMEM)
    vmem = pl.BlockSpec(memory_space=pltpu.VMEM)
    anywhere = pl.BlockSpec(memory_space=pltpu.HBM)
    return pl.pallas_call(
        project_kernel,
        out_shape=jax.ShapeDtypeStruct((rows, width), dtype),
        in_specs=[smem] + [anywhere] * (len(pieces) + len(weights)),
        out_specs=vmem,
        scratch_shapes=[
            pltpu.VMEM((rows, 2 * depth), BF16),
            pltpu.VMEM((2, depth, width), BF16),
            pltpu.SemaphoreType.DMA((4,)),
            pltpu.SemaphoreType.DMA((2,)),
        ],
        compiler_params=pltpu.CompilerParams(vmem_limit_bytes=16 << 20),
        cost_estimate=pl.CostEstimate(
            flops=4 * rows * depth * width, bytes_accessed=4 * depth * width * 2, transcendentals=0
        ),
        name="project",
    )(scalars, *pieces, *weights)


def scalars_of(*values):
    return jnp.stack([jnp.asarray(v, jnp.int32) for v in values])


def line_local(
    sizes,
    latents,
    w_qkv,
    w_out,
    query_gain,
    key_gain,
    mod_shift,
    mod_scale,
    mod_gate,
    block_list,
    block_live,
    key_valid,
):
    ny, nz, nx, nc = sizes
    y, z, x, c = (lax.axis_index(a) for a in AXES)

    def move(array, target):
        pairs = []
        for yy in range(ny):
            for zz in range(nz):
                for xx in range(nx):
                    for cc in range(nc):
                        to = target(yy, zz, xx, cc)
                        if to is not None:
                            flat = lambda p: ((p[0] * nz + p[1]) * nx + p[2]) * nc + p[3]
                            pairs.append((flat((yy, zz, xx, cc)), flat(to)))
        return lax.ppermute(array, AXES, pairs)

    def owns(zz, cc):
        return zz % 2 == cc

    def home(zz, cc):
        return zz // 2 == cc

    def mid(zz):
        return zz in (1, 2)

    def to_core(yy, zz, xx, cc):
        return (yy, zz, xx, 1 - cc)

    def to_column(who=lambda zz, cc: True):
        return lambda yy, zz, xx, cc: (yy, zz, 1 - xx, cc) if who(zz, cc) else None

    def to_replica(who=lambda zz, cc: True):
        return lambda yy, zz, xx, cc: (1 - yy, zz, xx, cc) if who(zz, cc) else None

    def else_core(real, left_out=lambda zz, cc: False):
        def target(yy, zz, xx, cc):
            to = real(yy, zz, xx, cc)
            if to is None and not left_out(zz, cc):
                return to_core(yy, zz, xx, cc)
            return to

        return target

    own = z % 2 == c
    at_home = z // 2 == c
    is_mid = (z == 1) | (z == 2)
    pair = z // 2
    parity = z % 2
    near, far = 2 * pair + c, 2 * (1 - pair) + c
    near_o, far_o = 2 * pair + 1 - c, 2 * (1 - pair) + 1 - c

    depth, _, heads_here, hd = w_qkv.shape
    heads = heads_here * nc // nz
    half = depth // 2
    w_t = jnp.transpose(w_qkv, (1, 2, 0, 3))
    wo = w_out.reshape(heads_here * hd, w_out.shape[2])

    def mid_own(zz, cc):
        return mid(zz) and owns(zz, cc)

    def mid_rest(zz, cc):
        return mid(zz) and not owns(zz, cc)

    def end_own(zz, cc):
        return not mid(zz) and owns(zz, cc)

    def end_rest(zz, cc):
        return not mid(zz) and not owns(zz, cc)

    def across(who):
        return lambda yy, zz, xx, cc: (yy, 3 - zz, xx, cc) if who(zz, cc) else None

    def outward(who):
        return lambda yy, zz, xx, cc: (yy, zz ^ 1, xx, cc) if who(zz, cc) else None

    n_mine = norm_rows(latents, mod_shift, mod_scale, x)
    r1 = move(n_mine, else_core(outward(owns)))
    r2a = move(n_mine, else_core(across(mid_own)))

    slot_a = jnp.where(at_home, 1 - parity, parity)
    slot_b = jnp.where(at_home, parity, 1 - parity)
    msg_a = lax.dynamic_slice(w_t, (0, slot_a * heads, y * half, 0), (3, heads, half, hd))
    msg_b = lax.dynamic_slice(w_t, (0, slot_b * heads, y * half, 0), (3, heads, half, hd))
    z_a = move(msg_a, lambda yy, zz, xx, cc: (yy, zz ^ 1, xx, 1) if home(zz, cc) else (yy, zz ^ 2, xx, 0))
    z_b = move(msg_b, lambda yy, zz, xx, cc: None if home(zz, cc) else (yy, zz ^ 3, xx, zz // 2))

    tile_ids = jnp.arange(nz, dtype=jnp.int32)
    hits = jnp.any((block_list[0][:, None] == tile_ids[None]) & (block_live[0][:, None] > 0), axis=0)
    flags = jnp.concatenate([key_valid, jnp.pad(hits.astype(jnp.int32), (0, 128 - nz))])[None]
    flags = jnp.concatenate(
        [flags]
        + [move(flags, lambda yy, zz, xx, cc, d=d: (yy, zz ^ d, xx, cc)) for d in range(1, nz)]
    )

    own_w = lax.dynamic_slice(w_t, (0, parity * heads, 0, 0), (3, heads, depth, hd))

    def mids(zz, cc):
        return mid(zz)

    def ends(zz, cc):
        return not mid(zz)

    r2b = move(r1, else_core(across(mid_rest)))
    x_r1 = move(r1, to_column())
    r3a = move(r2a, else_core(outward(mid_rest), end_rest))
    x_r2a = move(r2a, else_core(to_column(mid_rest), mids))
    r3b = move(r2b, else_core(outward(mid_own), end_own))
    x_r2b = move(r2b, else_core(to_column(mid_own), mids))
    x_r3a = move(r3a, else_core(to_column(end_own), ends))
    x_r3b = move(r3b, else_core(to_column(end_rest), ends))

    y_a = move(z_a, to_replica())
    c_a1 = move(z_a, to_core)
    c_own = move(own_w, to_core)
    y_b = move(z_b, to_replica(lambda zz, cc: not home(zz, cc)))
    c_b1 = move(z_b, to_core)
    c_a2 = move(y_a, to_core)
    c_b2 = move(y_b, to_core)
    weights = (z_a, y_a, c_a1, c_a2, own_w, c_own, z_b, y_b, c_b1, c_b2)
    sources = (
        jnp.where(c == 0, z ^ 2, z ^ 1),
        jnp.where(c == 0, z ^ 1, z ^ 2),
        z,
        z ^ 3,
        y,
        x,
        at_home,
    )

    def spread(step):
        def target(yy, zz, xx, cc):
            if cc == yy:
                return (yy, zz ^ step, xx, zz % 2)
            reached = (zz ^ step) % 2
            return None if cc != reached else to_core(yy, zz, xx, cc)

        return target

    s1 = move(wo, spread(1))

    def to_mids(yy, zz, xx, cc):
        if cc == yy:
            return (yy, 3 - zz if mid(zz) else zz ^ 2, xx, zz % 2)
        return None if mid(zz) else to_core(yy, zz, xx, cc)

    s2 = move(wo, to_mids)
    s3 = move(s2, outward(mids))
    c_f = move(wo, to_core)
    y_1 = move(s1, to_replica(lambda zz, cc: not owns(zz, cc)))
    y_2 = move(s2, else_core(to_replica(mids), lambda zz, cc: False))
    y_3 = move(s3, else_core(to_replica(end_own), ends))
    s4 = move(y_2, outward(mid_own))

    picks = (0, jnp.where(is_mid, jnp.where(own, 1, 0), jnp.where(own, 2, 3)))
    queries, kv = qkv_tiles(
        scalars_of(*sources, *picks),
        (((r1,), (x_r1,)), ((r2a, r2b, r3a, r3b), (x_r2a, x_r2b, x_r3a, x_r3b))),
        weights,
        query_gain,
        key_gain,
    )
    kv_other = move(kv, to_core)

    segments = (near, far, near_o, far_o)
    att_near, att_far = attend(scalars_of(*segments, *(s ^ z for s in segments)), queries, kv, kv_other, flags)
    p_far = move(att_far, lambda yy, zz, xx, cc: (yy, 2 * (1 - zz // 2) + cc, xx, zz % 2))
    p_near = move(att_near, else_core(outward(lambda zz, cc: not owns(zz, cc))))
    p_far_o = move(p_far, to_core)
    b_pair = move(p_near, to_core)

    pieces = (att_near, p_near, b_pair, p_far, p_far_o)
    blocks = (wo, c_f, s1, y_1, s2, y_2, s3, y_3, s3, s4)
    places = (own, z, z ^ 1, far, far_o)
    from_near = (jnp.where(own, 0, 1), jnp.where(own, c, y))
    from_far = (jnp.where(is_mid, 2, jnp.where(own, 3, 4)), y)
    near_stays = x == pair

    def project_block(near_block):
        chosen = [jnp.where(near_block, n, f) for n, f in zip(from_near, from_far)]
        return scalars_of(*places, *chosen)

    send = project(project_block(jnp.logical_not(near_stays)), pieces, blocks, BF16)
    got = move(send, to_column())
    keep = project(project_block(near_stays), pieces, blocks, F32)
    projected = keep + got.astype(F32)
    out_width = projected.shape[1]
    offset = (x * nc + c) * out_width
    latent_cols = lax.dynamic_slice_in_dim(latents, offset, out_width, 1).astype(F32)
    gate_cols = lax.dynamic_slice_in_dim(mod_gate, offset, out_width, 0)
    return (latent_cols + gate_cols * projected).astype(BF16)


def modulate(latents, mod_shift, mod_scale):
    x_float = latents.astype(F32)
    centre = x_float - jnp.mean(x_float, axis=-1, keepdims=True)
    spread = jnp.mean(centre * centre, axis=-1, keepdims=True)
    return (centre * lax.rsqrt(spread + EPS) * (1.0 + mod_scale) + mod_shift).astype(BF16)


def gather_local(
    latents,
    w_qkv,
    w_out,
    query_gain,
    key_gain,
    mod_shift,
    mod_scale,
    mod_gate,
    block_list,
    block_live,
    key_valid,
):
    gather = functools.partial(lax.all_gather, axis_name="seq", tiled=True)
    tok_rows = latents.shape[0]
    tile = tok_rows // block_list.shape[0]
    tiles_all = block_list.shape[0] * lax.axis_size("seq")
    normed = modulate(latents, mod_shift, mod_scale)
    qkv = jnp.einsum("td,dshe->tshe", normed, gather(w_qkv, axis=0), preferred_element_type=F32)
    queries = head_norm(qkv[:, 0], query_gain)
    keys = gather(head_norm(qkv[:, 1], key_gain), axis=0)
    values = gather(qkv[:, 2].astype(BF16), axis=0)
    key_ok = gather(key_valid, axis=0) > 0
    tile_ids = jnp.arange(tiles_all, dtype=jnp.int32)
    hits = jnp.any(
        (block_list[:, :, None] == tile_ids[None, None, :]) & (block_live[:, :, None] > 0), axis=1
    )
    allowed = jnp.repeat(jnp.repeat(hits, tile, axis=0), tile, axis=1) & key_ok[None, :]
    scores = jnp.einsum("qhe,khe->hqk", queries, keys, preferred_element_type=F32) / math.sqrt(
        queries.shape[-1]
    )
    masked = jnp.where(allowed[None], scores, NEG)
    weights = jnp.where(allowed[None], jnp.exp(masked - jnp.max(masked, axis=2, keepdims=True)), 0.0)
    total = jnp.sum(weights, axis=2)
    weighted = jnp.einsum("hqk,khe->qhe", weights.astype(BF16), values, preferred_element_type=F32)
    attended = (weighted / jnp.transpose(total)[:, :, None]).astype(BF16)
    head_terms = jnp.einsum("the,hec->tc", attended, gather(w_out, axis=2), preferred_element_type=F32)
    projected = lax.psum_scatter(
        head_terms.astype(BF16), ("tp", "sub"), scatter_dimension=1, tiled=True
    ).astype(F32)
    out_width = projected.shape[1]
    offset = lax.axis_index(("tp", "sub")) * out_width
    latent_cols = lax.dynamic_slice_in_dim(latents, offset, out_width, 1).astype(F32)
    gate_cols = lax.dynamic_slice_in_dim(mod_gate, offset, out_width, 0)
    return (latent_cols + gate_cols * projected).astype(BF16)


def solution(mesh):
    sizes = tuple(mesh.shape[a] for a in AXES)
    ny, nz, nx, nc = sizes
    line = ny == nx == nc == 2 and nz == nc * 2

    def local(*args):
        heads_here, block_list = args[1].shape[2], args[8]
        if line and heads_here % nc == 0 and block_list.shape[0] == 1:
            return line_local(sizes, *args)
        return gather_local(*args)

    in_specs = (
        P(("rep", "seq"), None),
        P("seq", None, ("tp", "sub"), None),
        P(("tp", "sub"), None, "seq"),
        P(),
        P(),
        P("rep"),
        P("rep"),
        P("rep"),
        P(("rep", "seq"), None),
        P(("rep", "seq"), None),
        P(("rep", "seq")),
    )
    out_specs = P(("rep", "seq"), ("tp", "sub"))
    return jax.shard_map(local, mesh=mesh, in_specs=in_specs, out_specs=out_specs, check_vma=False)
```

```python
import functools
import math

import jax
import jax.numpy as jnp
from jax import lax
from jax.experimental import pallas as pl
from jax.experimental.pallas import tpu as pltpu
from jax.sharding import PartitionSpec as P


AXES = ("rep", "seq", "tp", "sub")
EPS = 1e-06
NEG = -1e30
F32 = jnp.float32
BF16 = jnp.bfloat16


def norm_kernel(half_ref, x_ref, shift_ref, scale_ref, out_ref):
    x_float = x_ref[...].astype(F32)
    centre = x_float - jnp.mean(x_float, axis=-1, keepdims=True)
    spread = jnp.mean(centre * centre, axis=-1, keepdims=True)
    scaled = centre * lax.rsqrt(spread + EPS) * (1.0 + scale_ref[...])
    out_ref[...] = (scaled + shift_ref[...]).astype(BF16)


def norm_rows(latents, mod_shift, mod_scale, half):
    rows, width = latents.shape
    steps = 2
    block = rows // 2 // steps
    vector = pl.BlockSpec((1, width), lambda i, half_ref: (0, 0))
    return pl.pallas_call(
        norm_kernel,
        out_shape=jax.ShapeDtypeStruct((rows // 2, width), BF16),
        grid_spec=pltpu.PrefetchScalarGridSpec(
            num_scalar_prefetch=1,
            grid=(steps,),
            in_specs=[
                pl.BlockSpec((block, width), lambda i, half_ref: (half_ref[0] * steps + i, 0)),
                vector,
                vector,
            ],
            out_specs=pl.BlockSpec((block, width), lambda i, half_ref: (i, 0)),
        ),
        cost_estimate=pl.CostEstimate(flops=rows * width * 5, bytes_accessed=rows * width * 2, transcendentals=rows),
        name="norm_rows",
    )(half[None], latents, mod_shift[None], mod_scale[None])


def head_norm(raw, gain):
    square = jnp.mean(raw * raw, axis=-1, keepdims=True)
    return (raw * lax.rsqrt(square + EPS) * gain).astype(BF16)


def qkv_kernel(counts, sc_ref, *refs):
    tiles = []
    for count in counts:
        tiles.append((refs[:count], refs[count : 2 * count]))
        refs = refs[2 * count :]
    za, ya, ca1, ca2, own_w, own_c, zb, yb, cb1, cb2, gq_ref, gk_ref = refs[:12]
    q_ref, kv_ref, tok_ref, w_ref, acc_ref, gain_ref, tok_sem, w_sem, gain_sem = refs[12:]
    half_rows = tiles[0][0][0].shape[0]
    _, heads, depth, hd = za.shape
    col, rep, at_home = sc_ref[5], sc_ref[4], sc_ref[6] == 1
    bases = [pl.multiple_of(sc_ref[i] * (2 * depth), 128) for i in range(4)]

    def tok_copy(ref, block, tile, i):
        start = pl.multiple_of((col if i == 0 else 1 - col) * half_rows, 64)
        cols = pl.ds(bases[block], 2 * depth)
        dst = tok_ref.at[tile, pl.ds(start, half_rows), cols]
        return pltpu.make_async_copy(ref.at[:, cols], dst, tok_sem.at[block, tile, i])

    def w_copy(ref, block, i):
        if i is None:
            start, size, sem = bases[block], 2 * depth, w_sem.at[2 * block]
        else:
            start, size, sem = bases[block] + (rep if i == 0 else 1 - rep) * depth, depth, w_sem.at[2 * block + i]
        return pltpu.make_async_copy(ref, w_ref.at[:, :, pl.ds(pl.multiple_of(start, 128), size), :], sem)

    def when_home(home, away):
        @pl.when(at_home)
        def _():
            for copy in home:
                copy.start()

        @pl.when(jnp.logical_not(at_home))
        def _():
            for copy in away:
                copy.start()

        return home

    def fetch_weights(block):
        if block == 2:
            return when_home([w_copy(own_w, 2, None)], [w_copy(own_c, 2, None)])
        if block == 3:
            return when_home([w_copy(cb1, 3, 0), w_copy(cb2, 3, 1)], [w_copy(zb, 3, 0), w_copy(yb, 3, 1)])
        pair = (za, ya) if block == 0 else (ca1, ca2)
        copies = [w_copy(pair[0], block, 0), w_copy(pair[1], block, 1)]
        for copy in copies:
            copy.start()
        return copies

    def fetch(block):
        for tile, (mine, others) in enumerate(tiles):
            for i in range(counts[tile]):

                @pl.when(sc_ref[7 + tile] == i)
                def _():
                    tok_copy(mine[i], block, tile, 0).start()
                    tok_copy(others[i], block, tile, 1).start()

        waits = fetch_weights(block)
        return waits + [tok_copy(pairs[0], block, tile, i) for tile, t in enumerate(tiles) for i, pairs in enumerate(t)]

    gains = [pltpu.make_async_copy(r, gain_ref.at[i], gain_sem.at[i]) for i, r in enumerate((gq_ref, gk_ref))]
    waits = {0: fetch(0), 1: fetch(1)}
    for copy in gains:
        copy.start()
    for block in range(4):
        for copy in waits[block]:
            copy.wait()
        if block + 2 < 4:
            waits[block + 2] = fetch(block + 2)
        part = pl.ds(bases[block], 2 * depth)
        w = jnp.concatenate([w_ref[s, h, part, :] for s in range(3) for h in range(heads)], axis=1)
        for tile in range(2):
            term = jnp.dot(tok_ref[tile, :, part], w, preferred_element_type=F32)
            acc_ref[tile] = term if block == 0 else acc_ref[tile] + term

    for copy in gains:
        copy.wait()
    for tile in range(2):
        for h in range(heads):
            lanes = slice(h * hd, (h + 1) * hd)
            q_ref[tile, :, lanes] = head_norm(acc_ref[tile, :, lanes], gain_ref[0])
            kv_ref[tile, :, lanes] = head_norm(acc_ref[tile, :, (heads + h) * hd : (heads + h + 1) * hd], gain_ref[1])
        kv_ref[tile, :, heads * hd :] = acc_ref[tile, :, 2 * heads * hd :].astype(BF16)


def qkv_tiles(scalars, candidates, weights, query_gain, key_gain):
    half_rows, width = candidates[0][0][0].shape
    _, heads, _, hd = weights[0].shape
    rows, out = 2 * half_rows, heads * hd
    counts = tuple(len(mine) for mine, _ in candidates)
    tokens = [t for mine, others in candidates for t in (*mine, *others)]
    smem = pl.BlockSpec(memory_space=pltpu.SMEM)
    vmem = pl.BlockSpec(memory_space=pltpu.VMEM)
    anywhere = pl.BlockSpec(memory_space=pltpu.HBM)
    return pl.pallas_call(
        functools.partial(qkv_kernel, counts),
        out_shape=(
            jax.ShapeDtypeStruct((2, rows, out), BF16),
            jax.ShapeDtypeStruct((2, rows, 2 * out), BF16),
        ),
        in_specs=[smem] + [anywhere] * (len(tokens) + len(weights) + 2),
        out_specs=(vmem, vmem),
        scratch_shapes=[
            pltpu.VMEM((2, rows, width), BF16),
            pltpu.VMEM((3, heads, width, hd), BF16),
            pltpu.VMEM((2, rows, 3 * out), F32),
            pltpu.VMEM((2, 1, hd), F32),
            pltpu.SemaphoreType.DMA((4, 2, 2)),
            pltpu.SemaphoreType.DMA((8,)),
            pltpu.SemaphoreType.DMA((2,)),
        ],
        compiler_params=pltpu.CompilerParams(vmem_limit_bytes=24 << 20),
        cost_estimate=pl.CostEstimate(
            flops=12 * rows * width * out, bytes_accessed=width * 3 * out * 2, transcendentals=0
        ),
        name="qkv_tiles",
    )(scalars, *tokens, *weights, query_gain[None], key_gain[None])


def attend_kernel(sc_ref, q_ref, kv0, kv1, *refs):
    _, rows, width = q_ref.shape
    hd = 128
    heads = width // hd
    factor = math.log2(math.e) / math.sqrt(hd)
    flags, (near_ref, far_ref) = [r[...] for r in refs[:-2]], refs[-2:]
    segments = ((kv0, 0), (kv0, 1), (kv1, 0), (kv1, 1))

    def row(d):
        return functools.reduce(lambda a, i: jnp.where(d == i, flags[i], a), range(1, len(flags)), flags[0])

    rows_of = [row(sc_ref[4 + s]) for s in range(4)]
    biases = []
    for t in range(2):
        hits = rows_of[t][:, rows:]
        lane = lax.broadcasted_iota(jnp.int32, hits.shape, 1)
        bias = []
        for s in range(4):
            hit = jnp.sum(jnp.where(lane == sc_ref[s], hits, 0), axis=1, keepdims=True)
            bias.append(jnp.where(rows_of[s][:, :rows] * hit > 0, 0.0, NEG).astype(F32))
        biases.append(jnp.concatenate(bias, axis=1))
    for t, out_ref in ((1, far_ref), (0, near_ref)):
        for h in range(heads):
            lanes = slice(h * hd, (h + 1) * hd)
            keys = jnp.concatenate([r[s, :, lanes] for r, s in segments], axis=0)
            vals = jnp.concatenate([r[s, :, width + h * hd : width + (h + 1) * hd] for r, s in segments], axis=0)
            scores = lax.dot_general(
                q_ref[t, :, lanes], keys, (((1,), (1,)), ((), ())), preferred_element_type=F32
            )
            scores = scores * factor + biases[t]
            weights = jnp.exp2(scores - jnp.max(scores, axis=1, keepdims=True))
            total = jnp.sum(weights, axis=1, keepdims=True)
            added = jnp.dot(weights.astype(BF16), vals, preferred_element_type=F32)
            out_ref[:, lanes] = (added / total).astype(BF16)


def attend(scalars, queries, kv, kv_other, flags):
    _, rows, width = queries.shape
    smem = pl.BlockSpec(memory_space=pltpu.SMEM)
    vmem = pl.BlockSpec(memory_space=pltpu.VMEM)
    keys = 4 * rows
    shape = jax.ShapeDtypeStruct((rows, width), BF16)
    return pl.pallas_call(
        attend_kernel,
        out_shape=(shape, shape),
        in_specs=[smem] + [vmem] * (3 + len(flags)),
        out_specs=(vmem, vmem),
        compiler_params=pltpu.CompilerParams(vmem_limit_bytes=16 << 20),
        cost_estimate=pl.CostEstimate(
            flops=8 * rows * keys * width, bytes_accessed=8 * rows * width * 2, transcendentals=2 * rows * keys * width // 128
        ),
        name="attend",
    )(scalars, queries, kv, kv_other, *flags)


def project_kernel(sc_ref, an, pn, bp, f0, f1, *refs):
    firsts, seconds = refs[0:10:2], refs[1:10:2]
    out_ref, att_ref, w_ref, att_sem, w_sem = refs[10:]
    _, width = an.shape
    depth = w_ref.shape[1]

    def piece_copy(ref, i):
        lanes = pl.ds(pl.multiple_of(sc_ref[1 + i] * width, 128), width)
        return pltpu.make_async_copy(ref, att_ref.at[:, lanes], att_sem.at[i])

    @pl.when(sc_ref[0] == 1)
    def _():
        piece_copy(an, 0).start()
        piece_copy(pn, 1).start()

    @pl.when(sc_ref[0] == 0)
    def _():
        piece_copy(pn, 0).start()
        piece_copy(bp, 1).start()

    piece_copy(f0, 2).start()
    piece_copy(f1, 3).start()
    for i in range(5):

        @pl.when(sc_ref[5] == i)
        def _():
            pltpu.make_async_copy(firsts[i], w_ref.at[0], w_sem.at[0]).start()

    for i in range(4):
        piece_copy(f0, i).wait()
    for i in range(5):

        @pl.when(sc_ref[5] == i)
        def _():
            pltpu.make_async_copy(seconds[i], w_ref.at[1], w_sem.at[1]).start()

    terms = []
    for i in range(2):
        group = sc_ref[6] if i == 0 else 1 - sc_ref[6]
        pltpu.make_async_copy(firsts[0], w_ref.at[i], w_sem.at[i]).wait()
        part = att_ref[:, pl.ds(pl.multiple_of(group * depth, 128), depth)]
        terms.append(jnp.dot(part, w_ref[i], preferred_element_type=F32).astype(BF16).astype(F32))
    out_ref[...] = (terms[0] + terms[1]).astype(out_ref.dtype)


def project(scalars, pieces, weights, dtype):
    rows = pieces[0].shape[0]
    depth, width = weights[0].shape
    smem = pl.BlockSpec(memory_space=pltpu.SMEM)
    vmem = pl.BlockSpec(memory_space=pltpu.VMEM)
    anywhere = pl.BlockSpec(memory_space=pltpu.HBM)
    return pl.pallas_call(
        project_kernel,
        out_shape=jax.ShapeDtypeStruct((rows, width), dtype),
        in_specs=[smem, vmem] + [anywhere] * (len(pieces) - 1 + len(weights)),
        out_specs=vmem,
        scratch_shapes=[
            pltpu.VMEM((rows, 2 * depth), BF16),
            pltpu.VMEM((2, depth, width), BF16),
            pltpu.SemaphoreType.DMA((4,)),
            pltpu.SemaphoreType.DMA((2,)),
        ],
        compiler_params=pltpu.CompilerParams(vmem_limit_bytes=10 << 20),
        cost_estimate=pl.CostEstimate(
            flops=4 * rows * depth * width, bytes_accessed=4 * depth * width * 2, transcendentals=0
        ),
        name="project",
    )(scalars, *pieces, *weights)


def scalars_of(*values):
    return jnp.stack([jnp.asarray(v, jnp.int32) for v in values])


def line_local(
    sizes,
    latents,
    w_qkv,
    w_out,
    query_gain,
    key_gain,
    mod_shift,
    mod_scale,
    mod_gate,
    block_list,
    block_live,
    key_valid,
):
    ny, nz, nx, nc = sizes
    y, z, x, c = (lax.axis_index(a) for a in AXES)

    def move(array, target):
        pairs = []
        for yy in range(ny):
            for zz in range(nz):
                for xx in range(nx):
                    for cc in range(nc):
                        to = target(yy, zz, xx, cc)
                        if to is not None:
                            flat = lambda p: ((p[0] * nz + p[1]) * nx + p[2]) * nc + p[3]
                            pairs.append((flat((yy, zz, xx, cc)), flat(to)))
        return lax.ppermute(array, AXES, pairs)

    def owns(zz, cc):
        return zz % 2 == cc

    def home(zz, cc):
        return zz // 2 == cc

    def mid(zz):
        return zz in (1, 2)

    def to_core(yy, zz, xx, cc):
        return (yy, zz, xx, 1 - cc)

    def to_column(who=lambda zz, cc: True):
        return lambda yy, zz, xx, cc: (yy, zz, 1 - xx, cc) if who(zz, cc) else None

    def to_replica(who=lambda zz, cc: True):
        return lambda yy, zz, xx, cc: (1 - yy, zz, xx, cc) if who(zz, cc) else None

    def else_core(real, left_out=lambda zz, cc: False):
        def target(yy, zz, xx, cc):
            to = real(yy, zz, xx, cc)
            if to is None and not left_out(zz, cc):
                return to_core(yy, zz, xx, cc)
            return to

        return target

    own = z % 2 == c
    at_home = z // 2 == c
    is_mid = (z == 1) | (z == 2)
    pair = z // 2
    parity = z % 2
    near, far = 2 * pair + c, 2 * (1 - pair) + c
    near_o, far_o = 2 * pair + 1 - c, 2 * (1 - pair) + 1 - c

    depth, _, heads_here, hd = w_qkv.shape
    heads = heads_here * nc // nz
    half = depth // 2
    w_t = jnp.transpose(w_qkv, (1, 2, 0, 3))
    wo = w_out.reshape(heads_here * hd, w_out.shape[2])

    def mid_own(zz, cc):
        return mid(zz) and owns(zz, cc)

    def mid_rest(zz, cc):
        return mid(zz) and not owns(zz, cc)

    def end_own(zz, cc):
        return not mid(zz) and owns(zz, cc)

    def end_rest(zz, cc):
        return not mid(zz) and not owns(zz, cc)

    def across(who):
        return lambda yy, zz, xx, cc: (yy, 3 - zz, xx, cc) if who(zz, cc) else None

    def outward(who):
        return lambda yy, zz, xx, cc: (yy, zz ^ 1, xx, cc) if who(zz, cc) else None

    n_mine = norm_rows(latents, mod_shift, mod_scale, x)
    r1 = move(n_mine, else_core(outward(owns)))
    r2a = move(n_mine, else_core(across(mid_own)))

    slot_a = jnp.where(at_home, 1 - parity, parity)
    slot_b = jnp.where(at_home, parity, 1 - parity)
    msg_a = lax.dynamic_slice(w_t, (0, slot_a * heads, y * half, 0), (3, heads, half, hd))
    msg_b = lax.dynamic_slice(w_t, (0, slot_b * heads, y * half, 0), (3, heads, half, hd))
    z_a = move(msg_a, lambda yy, zz, xx, cc: (yy, zz ^ 1, xx, 1) if home(zz, cc) else (yy, zz ^ 2, xx, 0))
    z_b = move(msg_b, lambda yy, zz, xx, cc: None if home(zz, cc) else (yy, zz ^ 3, xx, zz // 2))

    tile_ids = jnp.arange(nz, dtype=jnp.int32)
    hits = jnp.any((block_list[0][:, None] == tile_ids[None]) & (block_live[0][:, None] > 0), axis=0)
    flags = jnp.concatenate([key_valid, jnp.pad(hits.astype(jnp.int32), (0, 128 - nz))])[None]
    flags = [flags] + [move(flags, lambda yy, zz, xx, cc, d=d: (yy, zz ^ d, xx, cc)) for d in range(1, nz)]

    own_w = lax.dynamic_slice(w_t, (0, parity * heads, 0, 0), (3, heads, depth, hd))

    def mids(zz, cc):
        return mid(zz)

    def ends(zz, cc):
        return not mid(zz)

    r2b = move(r1, else_core(across(mid_rest)))
    x_r1 = move(r1, to_column())
    r3a = move(r2a, else_core(outward(mid_rest), end_rest))
    x_r2a = move(r2a, else_core(to_column(mid_rest), mids))
    r3b = move(r2b, else_core(outward(mid_own), end_own))
    x_r2b = move(r2b, else_core(to_column(mid_own), mids))
    x_r3a = move(r3a, else_core(to_column(end_own), ends))
    x_r3b = move(r3b, else_core(to_column(end_rest), ends))

    y_a = move(z_a, to_replica())
    c_a1 = move(z_a, to_core)
    c_own = move(own_w, to_core)
    y_b = move(z_b, to_replica(lambda zz, cc: not home(zz, cc)))
    c_b1 = move(z_b, to_core)
    c_a2 = move(y_a, to_core)
    c_b2 = move(y_b, to_core)
    weights = (z_a, y_a, c_a1, c_a2, own_w, c_own, z_b, y_b, c_b1, c_b2)
    sources = (
        jnp.where(c == 0, z ^ 2, z ^ 1),
        jnp.where(c == 0, z ^ 1, z ^ 2),
        z,
        z ^ 3,
        y,
        x,
        at_home,
    )

    def spread(step):
        def target(yy, zz, xx, cc):
            if cc == yy:
                return (yy, zz ^ step, xx, zz % 2)
            reached = (zz ^ step) % 2
            return None if cc != reached else to_core(yy, zz, xx, cc)

        return target

    s1 = move(wo, spread(1))

    def to_mids(yy, zz, xx, cc):
        if cc == yy:
            return (yy, 3 - zz if mid(zz) else zz ^ 2, xx, zz % 2)
        return None if mid(zz) else to_core(yy, zz, xx, cc)

    s2 = move(wo, to_mids)
    s3 = move(s2, outward(mids))
    c_f = move(wo, to_core)
    y_1 = move(s1, to_replica(lambda zz, cc: not owns(zz, cc)))
    y_2 = move(s2, else_core(to_replica(mids), lambda zz, cc: False))
    y_3 = move(s3, else_core(to_replica(end_own), ends))
    s4 = move(y_2, outward(mid_own))

    picks = (0, jnp.where(is_mid, jnp.where(own, 1, 0), jnp.where(own, 2, 3)))
    queries, kv = qkv_tiles(
        scalars_of(*sources, *picks),
        (((r1,), (x_r1,)), ((r2a, r2b, r3a, r3b), (x_r2a, x_r2b, x_r3a, x_r3b))),
        weights,
        query_gain,
        key_gain,
    )
    kv_other = move(kv, to_core)

    segments = (near, far, near_o, far_o)
    att_near, att_far = attend(scalars_of(*segments, *(s ^ z for s in segments)), queries, kv, kv_other, flags)
    p_far = move(att_far, lambda yy, zz, xx, cc: (yy, 2 * (1 - zz // 2) + cc, xx, zz % 2))
    p_near = move(att_near, else_core(outward(lambda zz, cc: not owns(zz, cc))))
    p_far_o = move(p_far, to_core)
    b_pair = move(p_near, to_core)

    pieces = (att_near, p_near, b_pair, p_far, p_far_o)
    blocks = (wo, c_f, s1, y_1, s2, y_2, s3, y_3, s3, s4)
    places = (own, z, z ^ 1, far, far_o)
    from_near = (jnp.where(own, 0, 1), jnp.where(own, c, y))
    from_far = (jnp.where(is_mid, 2, jnp.where(own, 3, 4)), y)
    near_stays = x == pair

    def project_block(near_block):
        chosen = [jnp.where(near_block, n, f) for n, f in zip(from_near, from_far)]
        return scalars_of(*places, *chosen)

    send = project(project_block(jnp.logical_not(near_stays)), pieces, blocks, BF16)
    got = move(send, to_column())
    keep = project(project_block(near_stays), pieces, blocks, F32)
    projected = keep + got.astype(F32)
    out_width = projected.shape[1]
    offset = (x * nc + c) * out_width
    latent_cols = lax.dynamic_slice_in_dim(latents, offset, out_width, 1).astype(F32)
    gate_cols = lax.dynamic_slice_in_dim(mod_gate, offset, out_width, 0)
    return (latent_cols + gate_cols * projected).astype(BF16)


def modulate(latents, mod_shift, mod_scale):
    x_float = latents.astype(F32)
    centre = x_float - jnp.mean(x_float, axis=-1, keepdims=True)
    spread = jnp.mean(centre * centre, axis=-1, keepdims=True)
    return (centre * lax.rsqrt(spread + EPS) * (1.0 + mod_scale) + mod_shift).astype(BF16)


def gather_local(
    latents,
    w_qkv,
    w_out,
    query_gain,
    key_gain,
    mod_shift,
    mod_scale,
    mod_gate,
    block_list,
    block_live,
    key_valid,
):
    gather = functools.partial(lax.all_gather, axis_name="seq", tiled=True)
    tok_rows = latents.shape[0]
    tile = tok_rows // block_list.shape[0]
    tiles_all = block_list.shape[0] * lax.axis_size("seq")
    normed = modulate(latents, mod_shift, mod_scale)
    qkv = jnp.einsum("td,dshe->tshe", normed, gather(w_qkv, axis=0), preferred_element_type=F32)
    queries = head_norm(qkv[:, 0], query_gain)
    keys = gather(head_norm(qkv[:, 1], key_gain), axis=0)
    values = gather(qkv[:, 2].astype(BF16), axis=0)
    key_ok = gather(key_valid, axis=0) > 0
    tile_ids = jnp.arange(tiles_all, dtype=jnp.int32)
    hits = jnp.any(
        (block_list[:, :, None] == tile_ids[None, None, :]) & (block_live[:, :, None] > 0), axis=1
    )
    allowed = jnp.repeat(jnp.repeat(hits, tile, axis=0), tile, axis=1) & key_ok[None, :]
    scores = jnp.einsum("qhe,khe->hqk", queries, keys, preferred_element_type=F32) / math.sqrt(
        queries.shape[-1]
    )
    masked = jnp.where(allowed[None], scores, NEG)
    weights = jnp.where(allowed[None], jnp.exp(masked - jnp.max(masked, axis=2, keepdims=True)), 0.0)
    total = jnp.sum(weights, axis=2)
    weighted = jnp.einsum("hqk,khe->qhe", weights.astype(BF16), values, preferred_element_type=F32)
    attended = (weighted / jnp.transpose(total)[:, :, None]).astype(BF16)
    head_terms = jnp.einsum("the,hec->tc", attended, gather(w_out, axis=2), preferred_element_type=F32)
    projected = lax.psum_scatter(
        head_terms.astype(BF16), ("tp", "sub"), scatter_dimension=1, tiled=True
    ).astype(F32)
    out_width = projected.shape[1]
    offset = lax.axis_index(("tp", "sub")) * out_width
    latent_cols = lax.dynamic_slice_in_dim(latents, offset, out_width, 1).astype(F32)
    gate_cols = lax.dynamic_slice_in_dim(mod_gate, offset, out_width, 0)
    return (latent_cols + gate_cols * projected).astype(BF16)


def solution(mesh):
    sizes = tuple(mesh.shape[a] for a in AXES)
    ny, nz, nx, nc = sizes
    line = ny == nx == nc == 2 and nz == nc * 2

    def local(*args):
        heads_here, block_list = args[1].shape[2], args[8]
        if line and heads_here % nc == 0 and block_list.shape[0] == 1:
            return line_local(sizes, *args)
        return gather_local(*args)

    in_specs = (
        P(("rep", "seq"), None),
        P("seq", None, ("tp", "sub"), None),
        P(("tp", "sub"), None, "seq"),
        P(),
        P(),
        P("rep"),
        P("rep"),
        P("rep"),
        P(("rep", "seq"), None),
        P(("rep", "seq"), None),
        P(("rep", "seq")),
    )
    out_specs = P(("rep", "seq"), ("tp", "sub"))
    return jax.shard_map(local, mesh=mesh, in_specs=in_specs, out_specs=out_specs, check_vma=False)
```

```python
import functools
import math

import jax
import jax.numpy as jnp
from jax import lax
from jax.experimental import pallas as pl
from jax.experimental.pallas import tpu as pltpu
from jax.sharding import PartitionSpec as P


AXES = ("rep", "seq", "tp", "sub")
EPS = 1e-06
NEG = -1e30
F32 = jnp.float32
BF16 = jnp.bfloat16


def norm_kernel(half_ref, x_ref, shift_ref, scale_ref, out_ref):
    x_float = x_ref[...].astype(F32)
    centre = x_float - jnp.mean(x_float, axis=-1, keepdims=True)
    spread = jnp.mean(centre * centre, axis=-1, keepdims=True)
    scaled = centre * lax.rsqrt(spread + EPS) * (1.0 + scale_ref[...])
    out_ref[...] = (scaled + shift_ref[...]).astype(BF16)


def norm_rows(latents, mod_shift, mod_scale, half):
    rows, width = latents.shape
    steps = 2
    block = rows // 2 // steps
    vector = pl.BlockSpec((1, width), lambda i, half_ref: (0, 0))
    return pl.pallas_call(
        norm_kernel,
        out_shape=jax.ShapeDtypeStruct((rows // 2, width), BF16),
        grid_spec=pltpu.PrefetchScalarGridSpec(
            num_scalar_prefetch=1,
            grid=(steps,),
            in_specs=[
                pl.BlockSpec((block, width), lambda i, half_ref: (half_ref[0] * steps + i, 0)),
                vector,
                vector,
            ],
            out_specs=pl.BlockSpec((block, width), lambda i, half_ref: (i, 0)),
        ),
        cost_estimate=pl.CostEstimate(flops=rows * width * 5, bytes_accessed=rows * width * 2, transcendentals=rows),
        name="norm_rows",
    )(half[None], latents, mod_shift[None], mod_scale[None])


def head_norm(raw, gain):
    square = jnp.mean(raw * raw, axis=-1, keepdims=True)
    return (raw * lax.rsqrt(square + EPS) * gain).astype(BF16)


def qkv_kernel(counts, sc_ref, *refs):
    tiles = []
    for count in counts:
        tiles.append((refs[:count], refs[count : 2 * count]))
        refs = refs[2 * count :]
    za, ya, ca1, ca2, own_w, own_c, zb, yb, cb1, cb2, gq_ref, gk_ref = refs[:12]
    q_ref, kv_ref, tok_ref, w_ref, acc_ref, gain_ref, tok_sem, w_sem, gain_sem = refs[12:]
    half_rows = tiles[0][0][0].shape[0]
    _, heads, depth, hd = za.shape
    col, rep, at_home = sc_ref[5], sc_ref[4], sc_ref[6] == 1
    bases = [pl.multiple_of(sc_ref[i] * (2 * depth), 128) for i in range(4)]

    def tok_copy(ref, block, tile, i):
        start = pl.multiple_of((col if i == 0 else 1 - col) * half_rows, 64)
        cols = pl.ds(bases[block], 2 * depth)
        dst = tok_ref.at[tile, pl.ds(start, half_rows), cols]
        return pltpu.make_async_copy(ref.at[:, cols], dst, tok_sem.at[block, tile, i])

    def w_copy(ref, block, i):
        if i is None:
            start, size, sem = bases[block], 2 * depth, w_sem.at[2 * block]
        else:
            start, size, sem = bases[block] + (rep if i == 0 else 1 - rep) * depth, depth, w_sem.at[2 * block + i]
        return pltpu.make_async_copy(ref, w_ref.at[:, :, pl.ds(pl.multiple_of(start, 128), size), :], sem)

    def when_home(home, away):
        @pl.when(at_home)
        def _():
            for copy in home:
                copy.start()

        @pl.when(jnp.logical_not(at_home))
        def _():
            for copy in away:
                copy.start()

        return home

    def fetch_weights(block):
        if block == 2:
            return when_home([w_copy(own_w, 2, None)], [w_copy(own_c, 2, None)])
        if block == 3:
            return when_home([w_copy(cb1, 3, 0), w_copy(cb2, 3, 1)], [w_copy(zb, 3, 0), w_copy(yb, 3, 1)])
        pair = (za, ya) if block == 0 else (ca1, ca2)
        copies = [w_copy(pair[0], block, 0), w_copy(pair[1], block, 1)]
        for copy in copies:
            copy.start()
        return copies

    def fetch(block):
        for tile, (mine, others) in enumerate(tiles):
            for i in range(counts[tile]):

                @pl.when(sc_ref[7 + tile] == i)
                def _():
                    tok_copy(mine[i], block, tile, 0).start()
                    tok_copy(others[i], block, tile, 1).start()

        waits = fetch_weights(block)
        return waits + [tok_copy(pairs[0], block, tile, i) for tile, t in enumerate(tiles) for i, pairs in enumerate(t)]

    gains = [pltpu.make_async_copy(r, gain_ref.at[i], gain_sem.at[i]) for i, r in enumerate((gq_ref, gk_ref))]
    waits = {0: fetch(0), 1: fetch(1)}
    for copy in gains:
        copy.start()
    for block in range(4):
        for copy in waits[block]:
            copy.wait()
        if block + 2 < 4:
            waits[block + 2] = fetch(block + 2)
        part = pl.ds(bases[block], 2 * depth)
        w = jnp.concatenate([w_ref[s, h, part, :] for s in range(3) for h in range(heads)], axis=1)
        for tile in range(2):
            term = jnp.dot(tok_ref[tile, :, part], w, preferred_element_type=F32)
            acc_ref[tile] = term if block == 0 else acc_ref[tile] + term

    for copy in gains:
        copy.wait()
    for tile in range(2):
        for h in range(heads):
            lanes = slice(h * hd, (h + 1) * hd)
            q_ref[tile, :, lanes] = head_norm(acc_ref[tile, :, lanes], gain_ref[0])
            kv_ref[tile, :, lanes] = head_norm(acc_ref[tile, :, (heads + h) * hd : (heads + h + 1) * hd], gain_ref[1])
        kv_ref[tile, :, heads * hd :] = acc_ref[tile, :, 2 * heads * hd :].astype(BF16)


def qkv_tiles(scalars, candidates, weights, query_gain, key_gain):
    half_rows, width = candidates[0][0][0].shape
    _, heads, _, hd = weights[0].shape
    rows, out = 2 * half_rows, heads * hd
    counts = tuple(len(mine) for mine, _ in candidates)
    tokens = [t for mine, others in candidates for t in (*mine, *others)]
    smem = pl.BlockSpec(memory_space=pltpu.SMEM)
    vmem = pl.BlockSpec(memory_space=pltpu.VMEM)
    anywhere = pl.BlockSpec(memory_space=pltpu.HBM)
    return pl.pallas_call(
        functools.partial(qkv_kernel, counts),
        out_shape=(
            jax.ShapeDtypeStruct((2, rows, out), BF16),
            jax.ShapeDtypeStruct((2, rows, 2 * out), BF16),
        ),
        in_specs=[smem] + [anywhere] * (len(tokens) + len(weights) + 2),
        out_specs=(vmem, vmem),
        scratch_shapes=[
            pltpu.VMEM((2, rows, width), BF16),
            pltpu.VMEM((3, heads, width, hd), BF16),
            pltpu.VMEM((2, rows, 3 * out), F32),
            pltpu.VMEM((2, 1, hd), F32),
            pltpu.SemaphoreType.DMA((4, 2, 2)),
            pltpu.SemaphoreType.DMA((8,)),
            pltpu.SemaphoreType.DMA((2,)),
        ],
        compiler_params=pltpu.CompilerParams(vmem_limit_bytes=24 << 20),
        cost_estimate=pl.CostEstimate(
            flops=12 * rows * width * out, bytes_accessed=width * 3 * out * 2, transcendentals=0
        ),
        name="qkv_tiles",
    )(scalars, *tokens, *weights, query_gain[None], key_gain[None])


def attend_kernel(sc_ref, q_ref, kv0, kv1, *refs):
    _, rows, width = q_ref.shape
    hd = 128
    heads = width // hd
    factor = math.log2(math.e) / math.sqrt(hd)
    flags, (near_ref, far_ref) = [r[...] for r in refs[:-2]], refs[-2:]
    segments = ((kv0, 0), (kv0, 1), (kv1, 0), (kv1, 1))

    def row(d):
        return functools.reduce(lambda a, i: jnp.where(d == i, flags[i], a), range(1, len(flags)), flags[0])

    rows_of = [row(sc_ref[4 + s]) for s in range(4)]
    biases = []
    for t in range(2):
        hits = rows_of[t][:, rows:]
        lane = lax.broadcasted_iota(jnp.int32, hits.shape, 1)
        bias = []
        for s in range(4):
            hit = jnp.sum(jnp.where(lane == sc_ref[s], hits, 0), axis=1, keepdims=True)
            bias.append(jnp.where(rows_of[s][:, :rows] * hit > 0, 0.0, NEG).astype(F32))
        biases.append(jnp.concatenate(bias, axis=1))
    for t, out_ref in ((1, far_ref), (0, near_ref)):
        for h in range(heads):
            lanes = slice(h * hd, (h + 1) * hd)
            keys = jnp.concatenate([r[s, :, lanes] for r, s in segments], axis=0)
            vals = jnp.concatenate([r[s, :, width + h * hd : width + (h + 1) * hd] for r, s in segments], axis=0)
            scores = lax.dot_general(
                q_ref[t, :, lanes], keys, (((1,), (1,)), ((), ())), preferred_element_type=F32
            )
            scores = scores * factor + biases[t]
            weights = jnp.exp2(scores - jnp.max(scores, axis=1, keepdims=True))
            total = jnp.sum(weights, axis=1, keepdims=True)
            added = jnp.dot(weights.astype(BF16), vals, preferred_element_type=F32)
            out_ref[:, lanes] = (added / total).astype(BF16)


def attend(scalars, queries, kv, kv_other, flags):
    _, rows, width = queries.shape
    smem = pl.BlockSpec(memory_space=pltpu.SMEM)
    vmem = pl.BlockSpec(memory_space=pltpu.VMEM)
    keys = 4 * rows
    shape = jax.ShapeDtypeStruct((rows, width), BF16)
    return pl.pallas_call(
        attend_kernel,
        out_shape=(shape, shape),
        in_specs=[smem] + [vmem] * (3 + len(flags)),
        out_specs=(vmem, vmem),
        compiler_params=pltpu.CompilerParams(vmem_limit_bytes=16 << 20),
        cost_estimate=pl.CostEstimate(
            flops=8 * rows * keys * width, bytes_accessed=8 * rows * width * 2, transcendentals=2 * rows * keys * width // 128
        ),
        name="attend",
    )(scalars, queries, kv, kv_other, *flags)


def project_kernel(sc_ref, an, pn, bp, f0, f1, *refs):
    firsts, seconds = refs[0:10:2], refs[1:10:2]
    out_ref, att_ref, w_ref, att_sem, w_sem = refs[10:]
    _, width = an.shape
    depth = w_ref.shape[1]

    def piece_copy(ref, i):
        lanes = pl.ds(pl.multiple_of(sc_ref[1 + i] * width, 128), width)
        return pltpu.make_async_copy(ref, att_ref.at[:, lanes], att_sem.at[i])

    @pl.when(sc_ref[0] == 1)
    def _():
        piece_copy(an, 0).start()
        piece_copy(pn, 1).start()

    @pl.when(sc_ref[0] == 0)
    def _():
        piece_copy(pn, 0).start()
        piece_copy(bp, 1).start()

    piece_copy(f0, 2).start()
    piece_copy(f1, 3).start()
    for i in range(5):

        @pl.when(sc_ref[5] == i)
        def _():
            pltpu.make_async_copy(firsts[i], w_ref.at[0], w_sem.at[0]).start()

    for i in range(4):
        piece_copy(f0, i).wait()
    for i in range(5):

        @pl.when(sc_ref[5] == i)
        def _():
            pltpu.make_async_copy(seconds[i], w_ref.at[1], w_sem.at[1]).start()

    terms = []
    for i in range(2):
        group = sc_ref[6] if i == 0 else 1 - sc_ref[6]
        pltpu.make_async_copy(firsts[0], w_ref.at[i], w_sem.at[i]).wait()
        part = att_ref[:, pl.ds(pl.multiple_of(group * depth, 128), depth)]
        terms.append(jnp.dot(part, w_ref[i], preferred_element_type=F32).astype(BF16).astype(F32))
    out_ref[...] = (terms[0] + terms[1]).astype(out_ref.dtype)


def project(scalars, pieces, weights, dtype):
    rows = pieces[0].shape[0]
    depth, width = weights[0].shape
    smem = pl.BlockSpec(memory_space=pltpu.SMEM)
    vmem = pl.BlockSpec(memory_space=pltpu.VMEM)
    anywhere = pl.BlockSpec(memory_space=pltpu.HBM)
    return pl.pallas_call(
        project_kernel,
        out_shape=jax.ShapeDtypeStruct((rows, width), dtype),
        in_specs=[smem, vmem] + [anywhere] * (len(pieces) - 1 + len(weights)),
        out_specs=vmem,
        scratch_shapes=[
            pltpu.VMEM((rows, 2 * depth), BF16),
            pltpu.VMEM((2, depth, width), BF16),
            pltpu.SemaphoreType.DMA((4,)),
            pltpu.SemaphoreType.DMA((2,)),
        ],
        compiler_params=pltpu.CompilerParams(vmem_limit_bytes=10 << 20),
        cost_estimate=pl.CostEstimate(
            flops=4 * rows * depth * width, bytes_accessed=4 * depth * width * 2, transcendentals=0
        ),
        name="project",
    )(scalars, *pieces, *weights)


def scalars_of(*values):
    return jnp.stack([jnp.asarray(v, jnp.int32) for v in values])


def line_local(
    sizes,
    latents,
    w_qkv,
    w_out,
    query_gain,
    key_gain,
    mod_shift,
    mod_scale,
    mod_gate,
    block_list,
    block_live,
    key_valid,
):
    ny, nz, nx, nc = sizes
    y, z, x, c = (lax.axis_index(a) for a in AXES)

    def move(array, target):
        pairs = []
        for yy in range(ny):
            for zz in range(nz):
                for xx in range(nx):
                    for cc in range(nc):
                        to = target(yy, zz, xx, cc)
                        if to is not None:
                            flat = lambda p: ((p[0] * nz + p[1]) * nx + p[2]) * nc + p[3]
                            pairs.append((flat((yy, zz, xx, cc)), flat(to)))
        return lax.ppermute(array, AXES, pairs)

    def owns(zz, cc):
        return zz % 2 == cc

    def home(zz, cc):
        return zz // 2 == cc

    def mid(zz):
        return zz in (1, 2)

    def to_core(yy, zz, xx, cc):
        return (yy, zz, xx, 1 - cc)

    def to_column(who=lambda zz, cc: True):
        return lambda yy, zz, xx, cc: (yy, zz, 1 - xx, cc) if who(zz, cc) else None

    def to_replica(who=lambda zz, cc: True):
        return lambda yy, zz, xx, cc: (1 - yy, zz, xx, cc) if who(zz, cc) else None

    def else_core(real, left_out=lambda zz, cc: False):
        def target(yy, zz, xx, cc):
            to = real(yy, zz, xx, cc)
            if to is None and not left_out(zz, cc):
                return to_core(yy, zz, xx, cc)
            return to

        return target

    own = z % 2 == c
    at_home = z // 2 == c
    is_mid = (z == 1) | (z == 2)
    pair = z // 2
    parity = z % 2
    near, far = 2 * pair + c, 2 * (1 - pair) + c
    near_o, far_o = 2 * pair + 1 - c, 2 * (1 - pair) + 1 - c

    depth, _, heads_here, hd = w_qkv.shape
    heads = heads_here * nc // nz
    half = depth // 2
    w_t = jnp.transpose(w_qkv, (1, 2, 0, 3))
    wo = w_out.reshape(heads_here * hd, w_out.shape[2])

    def mid_own(zz, cc):
        return mid(zz) and owns(zz, cc)

    def mid_rest(zz, cc):
        return mid(zz) and not owns(zz, cc)

    def end_own(zz, cc):
        return not mid(zz) and owns(zz, cc)

    def end_rest(zz, cc):
        return not mid(zz) and not owns(zz, cc)

    def across(who):
        return lambda yy, zz, xx, cc: (yy, 3 - zz, xx, cc) if who(zz, cc) else None

    def outward(who):
        return lambda yy, zz, xx, cc: (yy, zz ^ 1, xx, cc) if who(zz, cc) else None

    n_mine = norm_rows(latents, mod_shift, mod_scale, x)
    r1 = move(n_mine, else_core(outward(owns)))
    r2a = move(n_mine, else_core(across(mid_own)))

    slot_a = jnp.where(at_home, 1 - parity, parity)
    slot_b = jnp.where(at_home, parity, 1 - parity)
    msg_a = lax.dynamic_slice(w_t, (0, slot_a * heads, y * half, 0), (3, heads, half, hd))
    msg_b = lax.dynamic_slice(w_t, (0, slot_b * heads, y * half, 0), (3, heads, half, hd))
    z_a = move(msg_a, lambda yy, zz, xx, cc: (yy, zz ^ 1, xx, 1) if home(zz, cc) else (yy, zz ^ 2, xx, 0))
    z_b = move(msg_b, lambda yy, zz, xx, cc: None if home(zz, cc) else (yy, zz ^ 3, xx, zz // 2))

    tile_ids = jnp.arange(nz, dtype=jnp.int32)
    hits = jnp.any((block_list[0][:, None] == tile_ids[None]) & (block_live[0][:, None] > 0), axis=0)
    flags = jnp.concatenate([key_valid, jnp.pad(hits.astype(jnp.int32), (0, 128 - nz))])[None]
    flags = [flags] + [move(flags, lambda yy, zz, xx, cc, d=d: (yy, zz ^ d, xx, cc)) for d in range(1, nz)]

    own_w = lax.dynamic_slice(w_t, (0, parity * heads, 0, 0), (3, heads, depth, hd))

    def mids(zz, cc):
        return mid(zz)

    def ends(zz, cc):
        return not mid(zz)

    r2b = move(r1, else_core(across(mid_rest)))
    x_r1 = move(r1, to_column())
    r3a = move(r2a, else_core(outward(mid_rest), end_rest))
    x_r2a = move(r2a, else_core(to_column(mid_rest), mids))
    r3b = move(r2b, else_core(outward(mid_own), end_own))
    x_r2b = move(r2b, else_core(to_column(mid_own), mids))
    x_r3a = move(r3a, else_core(to_column(end_own), ends))
    x_r3b = move(r3b, else_core(to_column(end_rest), ends))

    y_a = move(z_a, to_replica())
    c_a1 = move(z_a, to_core)
    c_own = move(own_w, to_core)
    y_b = move(z_b, to_replica(lambda zz, cc: not home(zz, cc)))
    c_b1 = move(z_b, to_core)
    c_a2 = move(y_a, to_core)
    c_b2 = move(y_b, to_core)
    weights = (z_a, y_a, c_a1, c_a2, own_w, c_own, z_b, y_b, c_b1, c_b2)
    sources = (
        jnp.where(c == 0, z ^ 2, z ^ 1),
        jnp.where(c == 0, z ^ 1, z ^ 2),
        z,
        z ^ 3,
        y,
        x,
        at_home,
    )

    def spread(step):
        def target(yy, zz, xx, cc):
            if cc == yy:
                return (yy, zz ^ step, xx, zz % 2)
            reached = (zz ^ step) % 2
            return None if cc != reached else to_core(yy, zz, xx, cc)

        return target

    s1 = move(wo, spread(1))

    def to_mids(yy, zz, xx, cc):
        if cc == yy:
            return (yy, 3 - zz if mid(zz) else zz ^ 2, xx, zz % 2)
        return None if mid(zz) else to_core(yy, zz, xx, cc)

    s2 = move(wo, to_mids)
    s3 = move(s2, outward(mids))
    c_f = move(wo, to_core)
    y_1 = move(s1, to_replica(lambda zz, cc: not owns(zz, cc)))
    y_2 = move(s2, else_core(to_replica(mids), lambda zz, cc: False))
    y_3 = move(s3, else_core(to_replica(end_own), ends))
    s4 = move(y_2, outward(mid_own))

    picks = (0, jnp.where(is_mid, jnp.where(own, 1, 0), jnp.where(own, 2, 3)))
    queries, kv = qkv_tiles(
        scalars_of(*sources, *picks),
        (((r1,), (x_r1,)), ((r2a, r2b, r3a, r3b), (x_r2a, x_r2b, x_r3a, x_r3b))),
        weights,
        query_gain,
        key_gain,
    )
    kv_other = move(kv, to_core)

    segments = (near, far, near_o, far_o)
    att_near, att_far = attend(scalars_of(*segments, *(s ^ z for s in segments)), queries, kv, kv_other, flags)
    p_far = move(att_far, lambda yy, zz, xx, cc: (yy, 2 * (1 - zz // 2) + cc, xx, zz % 2))
    p_near = move(att_near, else_core(outward(lambda zz, cc: not owns(zz, cc))))
    p_far_o = move(p_far, to_core)
    b_pair = move(p_near, to_core)

    pieces = (att_near, p_near, b_pair, p_far, p_far_o)
    blocks = (wo, c_f, s1, y_1, s2, y_2, s3, y_3, s3, s4)
    places = (own, z, z ^ 1, far, far_o)
    from_near = (jnp.where(own, 0, 1), jnp.where(own, c, y))
    from_far = (jnp.where(is_mid, 2, jnp.where(own, 3, 4)), y)
    near_stays = x == pair

    def project_block(near_block):
        chosen = [jnp.where(near_block, n, f) for n, f in zip(from_near, from_far)]
        return scalars_of(*places, *chosen)

    send = project(project_block(jnp.logical_not(near_stays)), pieces, blocks, BF16)
    got = move(send, to_column())
    keep = project(project_block(near_stays), pieces, blocks, F32)
    out_width = keep.shape[1]
    offset = (x * nc + c) * out_width
    latent_cols = lax.dynamic_slice_in_dim(latents, offset, out_width, 1).astype(F32)
    gate_cols = lax.dynamic_slice_in_dim(mod_gate, offset, out_width, 0)
    base = lax.optimization_barrier(latent_cols + gate_cols * keep)
    return (base + gate_cols * got.astype(F32)).astype(BF16)


def modulate(latents, mod_shift, mod_scale):
    x_float = latents.astype(F32)
    centre = x_float - jnp.mean(x_float, axis=-1, keepdims=True)
    spread = jnp.mean(centre * centre, axis=-1, keepdims=True)
    return (centre * lax.rsqrt(spread + EPS) * (1.0 + mod_scale) + mod_shift).astype(BF16)


def gather_local(
    latents,
    w_qkv,
    w_out,
    query_gain,
    key_gain,
    mod_shift,
    mod_scale,
    mod_gate,
    block_list,
    block_live,
    key_valid,
):
    gather = functools.partial(lax.all_gather, axis_name="seq", tiled=True)
    tok_rows = latents.shape[0]
    tile = tok_rows // block_list.shape[0]
    tiles_all = block_list.shape[0] * lax.axis_size("seq")
    normed = modulate(latents, mod_shift, mod_scale)
    qkv = jnp.einsum("td,dshe->tshe", normed, gather(w_qkv, axis=0), preferred_element_type=F32)
    queries = head_norm(qkv[:, 0], query_gain)
    keys = gather(head_norm(qkv[:, 1], key_gain), axis=0)
    values = gather(qkv[:, 2].astype(BF16), axis=0)
    key_ok = gather(key_valid, axis=0) > 0
    tile_ids = jnp.arange(tiles_all, dtype=jnp.int32)
    hits = jnp.any(
        (block_list[:, :, None] == tile_ids[None, None, :]) & (block_live[:, :, None] > 0), axis=1
    )
    allowed = jnp.repeat(jnp.repeat(hits, tile, axis=0), tile, axis=1) & key_ok[None, :]
    scores = jnp.einsum("qhe,khe->hqk", queries, keys, preferred_element_type=F32) / math.sqrt(
        queries.shape[-1]
    )
    masked = jnp.where(allowed[None], scores, NEG)
    weights = jnp.where(allowed[None], jnp.exp(masked - jnp.max(masked, axis=2, keepdims=True)), 0.0)
    total = jnp.sum(weights, axis=2)
    weighted = jnp.einsum("hqk,khe->qhe", weights.astype(BF16), values, preferred_element_type=F32)
    attended = (weighted / jnp.transpose(total)[:, :, None]).astype(BF16)
    head_terms = jnp.einsum("the,hec->tc", attended, gather(w_out, axis=2), preferred_element_type=F32)
    projected = lax.psum_scatter(
        head_terms.astype(BF16), ("tp", "sub"), scatter_dimension=1, tiled=True
    ).astype(F32)
    out_width = projected.shape[1]
    offset = lax.axis_index(("tp", "sub")) * out_width
    latent_cols = lax.dynamic_slice_in_dim(latents, offset, out_width, 1).astype(F32)
    gate_cols = lax.dynamic_slice_in_dim(mod_gate, offset, out_width, 0)
    return (latent_cols + gate_cols * projected).astype(BF16)


def solution(mesh):
    sizes = tuple(mesh.shape[a] for a in AXES)
    ny, nz, nx, nc = sizes
    line = ny == nx == nc == 2 and nz == nc * 2

    def local(*args):
        heads_here, block_list = args[1].shape[2], args[8]
        if line and heads_here % nc == 0 and block_list.shape[0] == 1:
            return line_local(sizes, *args)
        return gather_local(*args)

    in_specs = (
        P(("rep", "seq"), None),
        P("seq", None, ("tp", "sub"), None),
        P(("tp", "sub"), None, "seq"),
        P(),
        P(),
        P("rep"),
        P("rep"),
        P("rep"),
        P(("rep", "seq"), None),
        P(("rep", "seq"), None),
        P(("rep", "seq")),
    )
    out_specs = P(("rep", "seq"), ("tp", "sub"))
    return jax.shard_map(local, mesh=mesh, in_specs=in_specs, out_specs=out_specs, check_vma=False)
```
